512 devices in a mesh: section: 16 (over z), req: 4 (over y), tp: 8 (over x, core).
Axes of the slice: x: 4, y: 4, z: 16, core: 2. Of those that a mesh axis runs over, the one named last changes fastest.
Arguments:
- hidden: bfloat16 [4, 16, 64, 8192], P(None, 'section', 'req', 'tp'), may hold values from -6 to 6
- norm_gain: bfloat16 [16, 8192], P('section', 'tp'), may hold values from 0.099609375 to 1.8984375
- w_kv: bfloat16 [16, 8192, 2, 1024], P('section', None, None, 'tp'), may hold values from -0.0625 to 0.0625
- queries: bfloat16 [4, 16, 64, 8192], P(None, 'section', 'req', 'tp'), may hold values from -120 to 120
- cache_kv: bfloat16 [16, 64, 2, 128, 1024], P('section', 'req', None, None, 'tp'), may hold values from -4 to 4
- exits: int32 [4, 64], P(None, 'req'), may hold values from 0 to 16, as said below
- lengths: int32 [64], P('req'), may hold values from 2 to 124, as said below
Outputs:
- attn_out: bfloat16 [4, 16, 64, 8192], P(None, 'section', 'req', 'tp')
- new_kv: bfloat16 [4, 16, 64, 2, 1024], P(None, 'section', 'req', None, 'tp')
The draws below stay inside these ranges and needn't reach their ends.
Inputs may be any that keep to these rules, and one draw needn't show every extreme that they name: `exits`: in each step, among the 16 requests of each aligned block, no layer below 16 is named by more than 2 requests, some layer below 16 is named by exactly 2, and some request names 16. `lengths`: every aligned block of 16 requests holds a request of length 124.
All inputs are finite; a program needn't handle non-finite values.
Results may differ from the reference program's by a relative error of at most 0.0056.
Values may be sent and summed in bfloat16 or wider, within the bound.
No kernel may reach another device: no remote copies, remote signals or barrier semaphores. Data moves between devices by JAX's collectives and lax.ppermute only.
A program may use at most 64 MiB of HBM per device.

```python
import jax
import jax.numpy as jnp
from jax import lax

D = 8192
Q_HEADS = 64
KV_HEADS = 8
HEAD = 128
REQ_DEV = 16
CACHE = 128
STEPS = 4
EXIT_CAP = 2
LAYERS = 16
REQUESTS = 64


def shared_first_keys(key):
    return jnp.clip(jax.random.normal(jax.random.fold_in(key, 7), (LAYERS, REQUESTS, KV_HEADS, HEAD), jnp.float32), -4.0, 4.0)


def draw_cache_kv(key, part):
    first_keys = shared_first_keys(key)
    entries = jnp.clip(jax.random.normal(jax.random.fold_in(key, 11), (LAYERS, REQUESTS, 2, CACHE, KV_HEADS, HEAD), jnp.float32), -4.0, 4.0)
    entries = entries.at[:, :, 0, 0].set(first_keys)
    return entries.reshape(LAYERS, REQUESTS, 2, CACHE, KV_HEADS * HEAD).astype(jnp.bfloat16)


def draw_queries(key, part):
    groups = Q_HEADS // KV_HEADS
    entries = jnp.clip(jax.random.normal(jax.random.fold_in(key, 13), (STEPS, LAYERS, REQUESTS, KV_HEADS, groups, HEAD), jnp.float32), -4.0, 4.0)
    return entries.reshape(STEPS, LAYERS, REQUESTS, Q_HEADS * HEAD).astype(jnp.bfloat16)


def exit_block(block_key, block_number):
    drawn_layer = jax.random.randint(jax.random.fold_in(block_key, 1), (), 0, LAYERS).astype(jnp.int32)
    chosen = jnp.where(block_number == 0, 0, drawn_layer).astype(jnp.int32)
    base_pool = jnp.repeat(jnp.arange(0, LAYERS, dtype=jnp.int32), EXIT_CAP)
    base_pool = jnp.where(base_pool == chosen, LAYERS, base_pool).astype(jnp.int32)
    full_pool = jnp.concatenate([base_pool, jnp.full((REQ_DEV // 2,), LAYERS, jnp.int32)])
    full_pool = jax.random.permutation(jax.random.fold_in(block_key, 2), full_pool)
    picked = jnp.concatenate([full_pool[:REQ_DEV - EXIT_CAP - 1], jnp.zeros((EXIT_CAP,), jnp.int32) + chosen, jnp.full((1,), LAYERS, jnp.int32)])
    return jax.random.permutation(jax.random.fold_in(block_key, 3), picked)


def draw_exits(key, part):
    shards = REQUESTS // REQ_DEV
    block_keys = jax.random.split(jax.random.fold_in(key, 21), STEPS * shards)
    block_numbers = jnp.arange(STEPS * shards, dtype=jnp.int32)
    return jax.vmap(exit_block)(block_keys, block_numbers).reshape(STEPS, REQUESTS).astype(jnp.int32)


def draw_lengths(key, part):
    shards = REQUESTS // REQ_DEV
    drawn = jax.random.randint(jax.random.fold_in(key, 31), (shards, REQ_DEV), 2, CACHE - STEPS + 1)
    longest = jax.random.randint(jax.random.fold_in(key, 32), (shards, 1), 0, REQ_DEV)
    drawn = jnp.where(jnp.arange(REQ_DEV)[None, :] == longest, CACHE - STEPS, drawn)
    return drawn.reshape(REQUESTS).astype(jnp.int32)


def shard_levels(rng, dims, pieces, least, high):
    factor_of, own = 1.0, jax.random.fold_in(rng, 6)
    for axis_at, shards_of in pieces:
        draws = jnp.exp(jax.random.uniform(jax.random.fold_in(own, axis_at), (shards_of,), jnp.float32, least / len(pieces), high / len(pieces)))
        factor_of = factor_of * jnp.repeat(draws, dims[axis_at] // shards_of).reshape([-1 if axis == axis_at else 1 for axis in range(len(dims))])
    return factor_of


def bell_draw(rng, dims, scale, reach, cuts=(), held_as=jnp.bfloat16):
    array = scale * jax.random.normal(rng, dims, jnp.float32)
    if cuts:
        array = array * shard_levels(rng, dims, cuts, -0.22, 0.18)
    return jnp.clip(array, -reach, reach).astype(held_as)


def setup_inputs(seed: int = 0) -> dict:
    key_of = jax.random.split(jax.random.key(seed), 8)
    hidden = bell_draw(key_of[0], (STEPS, LAYERS, REQUESTS, D), 1.0, 6.0, ((1, 16), (2, 4), (3, 8)))
    norm_gain = jnp.clip(1.0 + 0.18 * jax.random.normal(key_of[1], (LAYERS, D), jnp.float32), 0.099609375, 1.8984375).astype(jnp.bfloat16)
    w_kv = bell_draw(key_of[2], (LAYERS, D, 2, KV_HEADS * HEAD), D ** -0.5, 0.0625, ((0, 16), (3, 8)))
    queries = draw_queries(jax.random.fold_in(key_of[7], 71), 0)
    cache_kv = draw_cache_kv(jax.random.fold_in(key_of[7], 71), 0)
    exits = draw_exits(jax.random.fold_in(key_of[7], 71), 0)
    lengths = draw_lengths(jax.random.fold_in(key_of[7], 71), 0)
    return dict(hidden=hidden, norm_gain=norm_gain, w_kv=w_kv, queries=queries, cache_kv=cache_kv, exits=exits, lengths=lengths)


EPSILON = 1e-05
ROPE_BASE = 500000.0

def apply_rotary(key_heads, positions):
    half_width = key_heads.shape[-1] // 2
    exponent = jnp.arange(half_width, dtype=jnp.float32) * (2.0 / key_heads.shape[-1])
    frequency = ROPE_BASE ** (-exponent)
    angles = positions.astype(jnp.float32)[..., None, None] * frequency
    cosine = jnp.cos(angles)
    sine_part = jnp.sin(angles)
    lower = key_heads[..., :half_width]
    upper = key_heads[..., half_width:]
    return jnp.concatenate([lower * cosine - upper * sine_part, upper * cosine + lower * sine_part], axis=-1)

def reference(hidden, norm_gain, w_kv, queries, cache_kv, exits, lengths):
    num_steps = hidden.shape[0]
    num_layers = hidden.shape[1]
    num_reqs = hidden.shape[2]
    width = hidden.shape[3]
    kv_width = w_kv.shape[-1]
    kv_heads = kv_width // HEAD
    groups = queries.shape[-1] // kv_width
    cache_len = cache_kv.shape[3]
    positions = lengths[None, :] + jnp.arange(num_steps, dtype=jnp.int32)[:, None]
    slot_ids = jnp.arange(cache_len, dtype=jnp.int32)
    step_ids = jnp.arange(num_steps, dtype=jnp.int32)[:, None]
    req_ids = jnp.arange(num_reqs, dtype=jnp.int32)[None, :]
    outputs = []
    written_kv = []
    for layer in range(num_layers):
        source = hidden[step_ids, jnp.minimum(exits, layer).astype(jnp.int32), req_ids]
        values_in = source.astype(jnp.float32)
        inverse = lax.rsqrt(lax.optimization_barrier(jnp.mean(values_in * values_in, axis=-1, keepdims=True)) + EPSILON)
        normed = (values_in * inverse * norm_gain[layer].astype(jnp.float32)).astype(jnp.bfloat16)
        pairs = jnp.dot(normed.reshape(num_steps * num_reqs, width), w_kv[layer].reshape(width, 2 * kv_width), preferred_element_type=jnp.float32)
        pairs = pairs.reshape(num_steps, num_reqs, 2, kv_heads, HEAD)
        new_keys = apply_rotary(pairs[:, :, 0], positions).astype(jnp.bfloat16)
        new_values = pairs[:, :, 1].astype(jnp.bfloat16)
        fresh_kv = jnp.stack([new_keys, new_values], axis=2).reshape(num_steps, num_reqs, 2, kv_width)
        written_kv.append(fresh_kv)
        kv_cache = cache_kv[layer]
        for step_index in range(num_steps):
            written = slot_ids[None, :] == positions[step_index][:, None]
            kv_cache = jnp.where(written[:, None, :, None], fresh_kv[step_index][:, :, None, :], kv_cache)
        all_keys = kv_cache[:, 0].reshape(num_reqs, cache_len, kv_heads, HEAD).astype(jnp.float32)
        all_values = kv_cache[:, 1].reshape(num_reqs, cache_len, kv_heads, HEAD).astype(jnp.float32)
        query_heads = queries[:, layer].reshape(num_steps, num_reqs, kv_heads, groups, HEAD).astype(jnp.float32)
        scores = jnp.einsum('trkgd,rckd->trkgc', query_heads, all_keys) * HEAD ** (-0.5)
        visible = slot_ids[None, None, :] <= positions[:, :, None]
        scores = jnp.where(visible[:, :, None, None, :], scores, -1e+30)
        top_score = lax.optimization_barrier(jnp.max(scores, axis=-1, keepdims=True))
        weights = jnp.exp(scores - top_score)
        weights = (weights / lax.optimization_barrier(jnp.sum(weights, axis=-1, keepdims=True))).astype(jnp.bfloat16)
        weights = lax.optimization_barrier(weights).astype(jnp.float32)
        attended = jnp.einsum('trkgc,rckd->trkgd', weights, all_values)
        live_mask = (layer < exits).astype(jnp.float32)
        attended = attended * live_mask[:, :, None, None, None]
        outputs.append(attended.reshape(num_steps, num_reqs, groups * kv_width).astype(jnp.bfloat16))
    return (jnp.stack(outputs, axis=1), jnp.stack(written_kv, axis=1))
```

```python
import jax
import jax.numpy as jnp
from jax import lax
from jax.sharding import PartitionSpec as P

D = 8192
HEAD = 128
EXIT_CAP = 2


EPSILON = 1e-05
ROPE_BASE = 500000.0


def apply_rotary(key_heads, positions):
    half_width = key_heads.shape[-1] // 2
    exponent = jnp.arange(half_width, dtype=jnp.float32) * (2.0 / key_heads.shape[-1])
    frequency = ROPE_BASE ** (-exponent)
    angles = positions.astype(jnp.float32)[..., None, None] * frequency
    cosine = jnp.cos(angles)
    sine_part = jnp.sin(angles)
    lower = key_heads[..., :half_width]
    upper = key_heads[..., half_width:]
    return jnp.concatenate(
        [lower * cosine - upper * sine_part, upper * cosine + lower * sine_part], axis=-1
    )


def spread(x, axis, count, groups=None):
    return lax.all_to_all(
        jnp.broadcast_to(x[None], (count,) + x.shape), axis, 0, 0, axis_index_groups=groups
    )


def source_rows(own_rows, exits, section_index, sections):
    steps, reqs, width = own_rows.shape
    rows = steps * reqs
    same = exits[:, :, None] == exits[:, None, :]
    earlier = jnp.arange(reqs)[None, None, :] < jnp.arange(reqs)[None, :, None]
    rank = jnp.sum((same & earlier).astype(jnp.int32), axis=-1)
    step_of = jnp.arange(steps, dtype=jnp.int32)[:, None]
    place = (step_of * EXIT_CAP + rank).reshape(rows)
    flat_exits = exits.reshape(rows)
    slots = steps * EXIT_CAP
    own_flat = own_rows.reshape(rows, width)
    slot_ids = jnp.arange(slots, dtype=jnp.int32)
    pick = (slot_ids[:, None] == place[None, :]) & (flat_exits == section_index)[None, :]
    outgoing = jnp.dot(
        pick.astype(jnp.bfloat16), own_flat, preferred_element_type=jnp.float32
    ).astype(jnp.bfloat16)
    arrived = spread(outgoing, "section", sections).reshape(sections * slots, width)
    gone = flat_exits < section_index
    all_ids = jnp.arange(sections * slots, dtype=jnp.int32)
    take = (all_ids[None, :] == (flat_exits * slots + place)[:, None]) & gone[:, None]
    taken = jnp.dot(
        take.astype(jnp.bfloat16), arrived, preferred_element_type=jnp.float32
    ).astype(jnp.bfloat16)
    return jnp.where(gone[:, None], taken, own_flat)


def local(hidden, norm_gain, w_kv, queries, cache_kv, exits, lengths):
    num_steps = hidden.shape[0]
    local_reqs = hidden.shape[2]
    rows = num_steps * local_reqs
    sections = lax.axis_size("section")
    section_index = lax.axis_index("section")
    parts = lax.axis_size("tp")
    chips = parts // 2
    core = lax.axis_index("tp") % 2
    source = source_rows(hidden[:, 0], exits, section_index, sections)
    sent = jnp.concatenate([source, jnp.broadcast_to(norm_gain, (8, norm_gain.shape[1]))], axis=0)
    same_core = [[2 * x + c for x in range(chips)] for c in range(2)]
    mine = spread(sent, "tp", chips, same_core)
    other = lax.ppermute(mine, "tp", [(i, i ^ 1) for i in range(parts)])
    even = jnp.where(core == 0, mine, other)
    odd = jnp.where(core == 0, other, mine)
    both = jnp.stack([even, odd], axis=1).reshape(parts, rows + 8, D // parts)
    raw = both[:, :rows].astype(jnp.float32)
    gain = both[:, rows].astype(jnp.float32)
    squares = jnp.sum(raw * raw, axis=(0, 2))
    inverse = lax.rsqrt(squares / D + EPSILON)
    normed = (raw * inverse[None, :, None] * gain[:, None, :]).astype(jnp.bfloat16)
    kv_local = w_kv.shape[-1]
    weight = w_kv[0].reshape(parts, D // parts, 2 * kv_local)
    kv_pairs = jnp.einsum("prd,pdk->rk", normed, weight, preferred_element_type=jnp.float32)
    local_heads = kv_local // HEAD
    kv_pairs = kv_pairs.reshape(num_steps, local_reqs, 2, local_heads, HEAD)
    positions = lengths[None, :] + jnp.arange(num_steps, dtype=jnp.int32)[:, None]
    new_keys = apply_rotary(kv_pairs[:, :, 0], positions).astype(jnp.bfloat16)
    new_values = kv_pairs[:, :, 1].astype(jnp.bfloat16)
    fresh_kv = jnp.stack([new_keys, new_values], axis=2).reshape(num_steps, local_reqs, 2, kv_local)
    kv_cache = cache_kv[0]
    cache_len = kv_cache.shape[2]
    slot_ids = jnp.arange(cache_len, dtype=jnp.int32)
    for step_index in range(num_steps):
        written = slot_ids[None, :] == positions[step_index][:, None]
        kv_cache = jnp.where(
            written[:, None, :, None], fresh_kv[step_index][:, :, None, :], kv_cache
        )
    all_keys = kv_cache[:, 0].reshape(local_reqs, cache_len, local_heads, HEAD)
    all_values = kv_cache[:, 1].reshape(local_reqs, cache_len, local_heads, HEAD)
    groups = queries.shape[-1] // kv_local
    query_heads = queries[:, 0].reshape(num_steps, local_reqs, local_heads, groups, HEAD)
    scores = jnp.einsum(
        "trkgd,rckd->trkgc", query_heads, all_keys, preferred_element_type=jnp.float32
    ) * HEAD ** (-0.5)
    visible = slot_ids[None, None, :] <= positions[:, :, None]
    scores = jnp.where(visible[:, :, None, None, :], scores, -1e30)
    top_score = jnp.max(scores, axis=-1, keepdims=True)
    weights = jnp.exp(scores - top_score)
    weights = (weights / jnp.sum(weights, axis=-1, keepdims=True)).astype(jnp.bfloat16)
    attended = jnp.einsum(
        "trkgc,rckd->trkgd", weights, all_values, preferred_element_type=jnp.float32
    )
    live_mask = (section_index < exits).astype(jnp.float32)
    attended = attended * live_mask[:, :, None, None, None]
    attended = attended.reshape(num_steps, 1, local_reqs, queries.shape[-1]).astype(jnp.bfloat16)
    return (attended, fresh_kv[:, None])


def solution(mesh):
    placed = (
        P(None, "section", "req", "tp"),
        P("section", "tp"),
        P("section", None, None, "tp"),
        P(None, "section", "req", "tp"),
        P("section", "req", None, None, "tp"),
        P(None, "req"),
        P("req"),
    )
    return jax.shard_map(
        local,
        mesh=mesh,
        in_specs=placed,
        out_specs=(P(None, "section", "req", "tp"), P(None, "section", "req", None, "tp")),
        check_vma=False,
    )
```

```python
import jax
import jax.numpy as jnp
from jax import lax
from jax.experimental import pallas as pl
from jax.experimental.pallas import tpu as pltpu
from jax.sharding import PartitionSpec as P

D = 8192
HEAD = 128
EXIT_CAP = 2
GAIN_ROWS = 8


EPSILON = 1e-05
ROPE_BASE = 500000.0
VMEM = pl.BlockSpec(memory_space=pltpu.VMEM)
SMEM = pl.BlockSpec(memory_space=pltpu.SMEM)


def iota(shape, axis):
    return lax.broadcasted_iota(jnp.int32, shape, axis)


def contract_last(a, b):
    return lax.dot_general(a, b, (((1,), (1,)), ((), ())), preferred_element_type=jnp.float32)


def leaving_kernel(reqs, section, exits_row, exits_column, own, out):
    rows = own.shape[0]
    slots = out.shape[1]
    by_row, by_column = exits_row[...], exits_column[...]
    first, second = iota((rows, rows), 0), iota((rows, rows), 1)
    earlier = (by_row == by_column) & (first < second) & (first // reqs == second // reqs)
    rank = jnp.sum(earlier.astype(jnp.float32), axis=0, keepdims=True).astype(jnp.int32)
    place = (iota((1, rows), 1) // reqs) * EXIT_CAP + rank
    pick = (iota((slots, rows), 0) == place) & (by_row == section[0])
    chosen = jnp.dot(
        pick.astype(jnp.float32).astype(jnp.bfloat16), own[...], preferred_element_type=jnp.float32
    ).astype(jnp.bfloat16)
    for k in range(out.shape[0]):
        out[k] = chosen


def ready_kernel(scale, lengths, weight, queries, cache, out_weight, out_old):
    step = pl.program_id(0)
    half = 128
    to, fro = iota((2 * half, 2 * half), 0), iota((2 * half, 2 * half), 1)
    split = (fro == jnp.where(to < half, 2 * to, 2 * (to - half) + 1)).astype(jnp.float32)
    split = split.astype(jnp.bfloat16)
    for j in range(weight.shape[0] // (2 * half)):
        pair = jnp.dot(
            split, weight[2 * half * j : 2 * half * (j + 1), :], preferred_element_type=jnp.float32
        ).astype(jnp.bfloat16)
        out_weight[0, half * j : half * (j + 1), 0:HEAD] = pair[:half]
        out_weight[0, half * j : half * (j + 1), HEAD : 2 * HEAD] = pair[half:]
    here = cache.shape[0]
    per = queries.shape[0] // here
    for k in range(here):
        length = lengths[step * here + k]
        span = slice(k * per, (k + 1) * per)
        scores = contract_last(queries[span, :], cache[k, 0]) * scale
        scores = jnp.where(iota(scores.shape, 1) < length, scores, -1e30)
        top = jnp.max(scores, axis=-1, keepdims=True)
        grown = jnp.exp(scores - top)
        total = jnp.sum(grown, axis=-1, keepdims=True)
        high = grown.astype(jnp.bfloat16)
        low = (grown - high.astype(jnp.float32)).astype(jnp.bfloat16)
        values = cache[k, 1]
        out_old[span, 0:HEAD] = jnp.dot(
            high, values, preferred_element_type=jnp.float32
        ) + jnp.dot(low, values, preferred_element_type=jnp.float32)
        out_old[span, HEAD : 2 * HEAD] = jnp.broadcast_to(top, (per, HEAD))
        out_old[span, 2 * HEAD : 3 * HEAD] = jnp.broadcast_to(total, (per, HEAD))


def place_kernel(take, kept, arrived, gain, out):
    rows = kept.shape[0]
    source = jnp.dot(take[...], arrived[...], preferred_element_type=jnp.float32)
    source = (source + kept[...].astype(jnp.float32)).astype(jnp.bfloat16)
    gains = jnp.broadcast_to(gain[...], (GAIN_ROWS, gain.shape[1]))
    for k in range(out.shape[0]):
        out[k, 0:rows, :] = source
        out[k, rows : rows + GAIN_ROWS, :] = gains


def finish_kernel(reqs, scale, core, mine, other, weight, queries, old, table, out_attn, out_kv):
    rows = queries.shape[0]
    chips = mine.shape[0]
    width = mine.shape[2]
    squares = jnp.zeros((rows, HEAD), jnp.float32)
    for held in (mine, other):
        for x in range(chips):
            for j in range(width // HEAD):
                value = held[x, 0:rows, HEAD * j : HEAD * (j + 1)].astype(jnp.float32)
                squares = squares + value * value
    mean = jnp.sum(squares, axis=-1, keepdims=True) / D
    inverse = lax.rsqrt(mean + EPSILON)
    pairs = jnp.zeros((rows, 2 * HEAD), jnp.float32)
    for held, parity in ((mine, core[0]), (other, 1 - core[0])):
        for x in range(chips):
            value = held[x, 0:rows, :].astype(jnp.float32)
            gain = held[x, rows : rows + 1, :].astype(jnp.float32)
            normed = (value * inverse * gain).astype(jnp.bfloat16)
            pairs = pairs + jnp.dot(
                normed, weight[2 * x + parity], preferred_element_type=jnp.float32
            )
    keys = pairs[:, :HEAD]
    turned = pltpu.roll(keys, HEAD // 2, 1)
    new_keys = (keys * table[0] + turned * table[1]).astype(jnp.bfloat16)
    new_values = pairs[:, HEAD:].astype(jnp.bfloat16)
    to, fro = iota((2 * rows, 2 * rows), 0), iota((2 * rows, 2 * rows), 1)
    weave = (fro == (to // 2) + rows * (to % 2)).astype(jnp.float32).astype(jnp.bfloat16)
    stacked = jnp.concatenate([new_keys, new_values], axis=0)
    out_kv[...] = jnp.dot(weave, stacked, preferred_element_type=jnp.float32).astype(jnp.bfloat16)
    by, of = iota((rows, rows), 0), iota((rows, rows), 1)
    seen = (by % reqs == of % reqs) & (of // reqs <= by // reqs)
    live = table[2]
    for g in range(old.shape[0]):
        span = slice(g * HEAD, (g + 1) * HEAD)
        scores = contract_last(queries[:, span], new_keys) * scale
        scores = jnp.where(seen, scores, -1e30)
        before, old_top, old_total = old[g, :, 0:HEAD], old[g, :, HEAD : HEAD + 1], old[g, :, 2 * HEAD : 2 * HEAD + 1]
        top = jnp.maximum(old_top, jnp.max(scores, axis=-1, keepdims=True))
        shrink = jnp.exp(old_top - top)
        grown = jnp.exp(scores - top)
        total = shrink * old_total + jnp.sum(grown, axis=-1, keepdims=True)
        fresh = (grown / total).astype(jnp.bfloat16)
        mixed = before * (shrink / total) + jnp.dot(
            fresh, new_values, preferred_element_type=jnp.float32
        )
        out_attn[:, span] = (mixed * live).astype(jnp.bfloat16)


def spread(x, axis, groups=None):
    return lax.all_to_all(x, axis, 0, 0, axis_index_groups=groups)


def local(hidden, norm_gain, w_kv, queries, cache_kv, exits, lengths):
    num_steps, _, local_reqs, width = hidden.shape
    rows = num_steps * local_reqs
    slots = num_steps * EXIT_CAP
    sections = lax.axis_size("section")
    section_index = lax.axis_index("section")
    parts = lax.axis_size("tp")
    chips = parts // 2
    core = lax.axis_index("tp") % 2
    kv_local = w_kv.shape[-1]
    cache_len = cache_kv.shape[3]
    groups = queries.shape[-1] // kv_local
    scale = HEAD ** (-0.5)

    own = hidden.reshape(rows, width)
    flat_exits = exits.reshape(rows)
    outgoing = pl.pallas_call(
        lambda *refs: leaving_kernel(local_reqs, *refs),
        out_shape=jax.ShapeDtypeStruct((sections, slots, width), jnp.bfloat16),
        in_specs=[SMEM, VMEM, VMEM, VMEM],
        out_specs=VMEM,
        name="leaving",
    )(section_index.reshape(1), flat_exits[None, :], flat_exits[:, None], own)
    arrived = spread(outgoing, "section").reshape(sections * slots, width)

    same = exits[:, :, None] == exits[:, None, :]
    earlier = jnp.arange(local_reqs)[None, None, :] < jnp.arange(local_reqs)[None, :, None]
    rank = jnp.sum((same & earlier).astype(jnp.int32), axis=-1)
    step_of = jnp.arange(num_steps, dtype=jnp.int32)[:, None]
    place = (step_of * EXIT_CAP + rank).reshape(rows)
    gone = flat_exits < section_index
    all_ids = jnp.arange(sections * slots, dtype=jnp.int32)
    take = (all_ids[None, :] == (flat_exits * slots + place)[:, None]) & gone[:, None]
    take = take.astype(jnp.bfloat16)
    kept = jnp.where(gone[:, None], jnp.zeros_like(own), own)
    positions = (lengths[None, :] + step_of).reshape(rows)
    exponent = jnp.arange(HEAD // 2, dtype=jnp.float32) * (2.0 / HEAD)
    angles = positions.astype(jnp.float32)[:, None] * ROPE_BASE ** (-exponent)
    cosine, sine = jnp.cos(angles), jnp.sin(angles)
    live = (section_index < flat_exits).astype(jnp.float32)
    table = jnp.stack(
        [
            jnp.concatenate([cosine, cosine], axis=-1),
            jnp.concatenate([-sine, sine], axis=-1),
            jnp.broadcast_to(live[:, None], (rows, HEAD)),
        ]
    )
    by_request = queries.reshape(num_steps, local_reqs, groups, HEAD).transpose(1, 0, 2, 3)
    here = local_reqs // parts
    weight, old = pl.pallas_call(
        lambda *refs: ready_kernel(scale, *refs),
        grid=(parts,),
        out_shape=(
            jax.ShapeDtypeStruct((parts, width, 2 * HEAD), jnp.bfloat16),
            jax.ShapeDtypeStruct((rows * groups, 3 * HEAD), jnp.float32),
        ),
        in_specs=[
            SMEM,
            pl.BlockSpec((2 * width, HEAD), lambda i: (i, 0)),
            pl.BlockSpec((here * num_steps * groups, HEAD), lambda i: (i, 0)),
            pl.BlockSpec((here, 2, cache_len, HEAD), lambda i: (i, 0, 0, 0)),
        ],
        out_specs=(
            pl.BlockSpec((1, width, 2 * HEAD), lambda i: (i, 0, 0)),
            pl.BlockSpec((here * num_steps * groups, 3 * HEAD), lambda i: (i, 0)),
        ),
        name="ready",
    )(
        lengths,
        w_kv.reshape(2 * D, HEAD),
        by_request.reshape(rows * groups, HEAD),
        cache_kv[0],
    )
    old = old.reshape(local_reqs, num_steps, groups, 3 * HEAD).transpose(2, 1, 0, 3)
    old = old.reshape(groups, rows, 3 * HEAD)

    weight, old, table, take, kept, arrived = lax.optimization_barrier(
        (weight, old, table, take, kept, arrived)
    )
    sent = pl.pallas_call(
        place_kernel,
        out_shape=jax.ShapeDtypeStruct((chips, rows + GAIN_ROWS, width), jnp.bfloat16),
        in_specs=[VMEM] * 4,
        out_specs=VMEM,
        name="place",
    )(take, kept, arrived, norm_gain)
    same_core = [[2 * x + c for x in range(chips)] for c in range(2)]
    mine = spread(sent, "tp", same_core)
    other = lax.ppermute(mine, "tp", [(i, i ^ 1) for i in range(parts)])

    attended, fresh = pl.pallas_call(
        lambda *refs: finish_kernel(local_reqs, scale, *refs),
        out_shape=(
            jax.ShapeDtypeStruct((rows, groups * HEAD), jnp.bfloat16),
            jax.ShapeDtypeStruct((2 * rows, HEAD), jnp.bfloat16),
        ),
        in_specs=[SMEM] + [VMEM] * 6,
        out_specs=(VMEM, VMEM),
        name="finish",
    )(core.reshape(1), mine, other, weight, queries.reshape(rows, groups * HEAD), old, table)
    return (
        attended.reshape(num_steps, 1, local_reqs, groups * HEAD),
        fresh.reshape(num_steps, 1, local_reqs, 2, kv_local),
    )


def solution(mesh):
    placed = (
        P(None, "section", "req", "tp"),
        P("section", "tp"),
        P("section", None, None, "tp"),
        P(None, "section", "req", "tp"),
        P("section", "req", None, None, "tp"),
        P(None, "req"),
        P("req"),
    )
    return jax.shard_map(
        local,
        mesh=mesh,
        in_specs=placed,
        out_specs=(P(None, "section", "req", "tp"), P(None, "section", "req", None, "tp")),
        check_vma=False,
    )
```

```python
import jax
import jax.numpy as jnp
from jax import lax
from jax.experimental import pallas as pl
from jax.experimental.pallas import tpu as pltpu
from jax.sharding import PartitionSpec as P

D = 8192
HEAD = 128
EXIT_CAP = 2
GAIN_ROWS = 8


EPSILON = 1e-05
ROPE_BASE = 500000.0
VMEM = pl.BlockSpec(memory_space=pltpu.VMEM)
SMEM = pl.BlockSpec(memory_space=pltpu.SMEM)


def iota(shape, axis):
    return lax.broadcasted_iota(jnp.int32, shape, axis)


def contract_last(a, b):
    return lax.dot_general(a, b, (((1,), (1,)), ((), ())), preferred_element_type=jnp.float32)


def as_bf16(mask):
    return mask.astype(jnp.float32).astype(jnp.bfloat16)


def exact(a, b):
    return jnp.dot(a, b, preferred_element_type=jnp.float32)


def ranks(same):
    reqs = same.shape[1]
    before = iota((reqs, reqs), 0) < iota((reqs, reqs), 1)
    return exact(as_bf16(same), as_bf16(before))


def leaving_kernel(section, exits, own, out):
    steps, reqs = exits.shape
    rows = own.shape[0]
    here = exits[...] == section[0]
    rank = ranks(here)
    picks = [here & (rank == k) for k in range(EXIT_CAP)]
    picks = jnp.concatenate([pick.astype(jnp.float32) for pick in picks], axis=0)
    widen = as_bf16(iota((reqs, rows), 0) == iota((reqs, rows), 1) % reqs)
    wide = exact(picks.astype(jnp.bfloat16), widen)
    slots = EXIT_CAP * steps
    match = iota((slots, rows), 0) % steps == iota((slots, rows), 1) // reqs
    wide = jnp.where(match, wide, 0.0).astype(jnp.bfloat16)
    chosen = exact(wide, own[...]).astype(jnp.bfloat16)
    for k in range(out.shape[0]):
        out[k] = chosen


def choose_kernel(section, exits, own, take, kept):
    steps, reqs = exits.shape
    rows, reach = take.shape
    slots = EXIT_CAP * steps
    layer = exits[...]
    rank = jnp.zeros((steps, reqs), jnp.float32)
    for e in range(reach // slots):
        same = layer == e
        rank = jnp.where(same, ranks(same), rank)
    gone = layer < section[0]
    slot = layer * slots + rank.astype(jnp.int32) * steps + iota((steps, reqs), 0)
    slot = jnp.where(gone, slot, -1).astype(jnp.float32)
    spread_steps = as_bf16(iota((rows, steps), 0) // reqs == iota((rows, steps), 1))
    column = exact(spread_steps, slot.astype(jnp.bfloat16))
    own_lane = iota((rows, reqs), 0) % reqs == iota((rows, reqs), 1)
    column = jnp.sum(jnp.where(own_lane, column, 0.0), axis=-1, keepdims=True)
    take[...] = as_bf16(column.astype(jnp.int32) == iota((rows, reach), 1))
    kept[...] = jnp.where(column >= 0.0, 0.0, own[...].astype(jnp.float32)).astype(jnp.bfloat16)


def split_kernel(weight, out):
    half = 128
    to, fro = iota((2 * half, 2 * half), 0), iota((2 * half, 2 * half), 1)
    split = as_bf16(fro == jnp.where(to < half, 2 * to, 2 * (to - half) + 1))
    for j in range(weight.shape[0] // (2 * half)):
        pair = exact(split, weight[2 * half * j : 2 * half * (j + 1), :]).astype(jnp.bfloat16)
        out[0, half * j : half * (j + 1), 0:HEAD] = pair[:half]
        out[0, half * j : half * (j + 1), HEAD : 2 * HEAD] = pair[half:]


def past_kernel(scale, lengths, queries, cache, out):
    reqs = cache.shape[0]
    per = queries.shape[0] // reqs
    groups = out.shape[0]
    for r in range(reqs):
        scores = contract_last(queries[r * per : (r + 1) * per, :], cache[r, 0]) * scale
        scores = jnp.where(iota(scores.shape, 1) < lengths[r], scores, -1e30)
        top = jnp.max(scores, axis=-1, keepdims=True)
        grown = jnp.exp(scores - top)
        total = jnp.sum(grown, axis=-1, keepdims=True)
        high = grown.astype(jnp.bfloat16)
        low = (grown - high.astype(jnp.float32)).astype(jnp.bfloat16)
        mixed = exact(high, cache[r, 1]) + exact(low, cache[r, 1])
        top = jnp.broadcast_to(top, (per, HEAD))
        total = jnp.broadcast_to(total, (per, HEAD))
        for t in range(per // groups):
            row = slice(t * reqs + r, t * reqs + r + 1)
            for g in range(groups):
                at = slice(t * groups + g, t * groups + g + 1)
                out[g, row, 0:HEAD] = mixed[at]
                out[g, row, HEAD : 2 * HEAD] = top[at]
                out[g, row, 2 * HEAD : 3 * HEAD] = total[at]


def place_kernel(take, kept, arrived, gain, out):
    rows = kept.shape[0]
    source = jnp.dot(take[...], arrived[...], preferred_element_type=jnp.float32)
    source = (source + kept[...].astype(jnp.float32)).astype(jnp.bfloat16)
    gains = jnp.broadcast_to(gain[...], (GAIN_ROWS, gain.shape[1]))
    for k in range(out.shape[0]):
        out[k, 0:rows, :] = source
        out[k, rows : rows + GAIN_ROWS, :] = gains


def finish_kernel(
    reqs, scale, core, mine, other, weight, queries, old, table, out_attn, out_kv, held_weight, sems
):
    rows = queries.shape[0]
    chips = mine.shape[0]
    width = mine.shape[2]
    order = [(mine, x, 2 * x + core[0]) for x in range(chips)]
    order += [(other, x, 2 * x + 1 - core[0]) for x in range(chips)]
    loads = [
        pltpu.make_async_copy(weight.at[part], held_weight.at[i], sems.at[i])
        for i, (_, _, part) in enumerate(order)
    ]
    for load in loads:
        load.start()
    squares = jnp.zeros((rows, HEAD), jnp.float32)
    for held in (mine, other):
        for x in range(chips):
            for j in range(width // HEAD):
                value = held[x, 0:rows, HEAD * j : HEAD * (j + 1)].astype(jnp.float32)
                squares = squares + value * value
    mean = jnp.sum(squares, axis=-1, keepdims=True) / D
    inverse = lax.rsqrt(mean + EPSILON)
    pairs = jnp.zeros((rows, 2 * HEAD), jnp.float32)
    for i, (held, x, _) in enumerate(order):
        value = held[x, 0:rows, :].astype(jnp.float32)
        gain = held[x, rows : rows + 1, :].astype(jnp.float32)
        normed = (value * inverse * gain).astype(jnp.bfloat16)
        loads[i].wait()
        pairs = pairs + exact(normed, held_weight[i])
    keys = pairs[:, :HEAD]
    turned = pltpu.roll(keys, HEAD // 2, 1)
    new_keys = (keys * table[0] + turned * table[1]).astype(jnp.bfloat16)
    new_values = pairs[:, HEAD:].astype(jnp.bfloat16)
    to, fro = iota((2 * rows, 2 * rows), 0), iota((2 * rows, 2 * rows), 1)
    weave = (fro == (to // 2) + rows * (to % 2)).astype(jnp.float32).astype(jnp.bfloat16)
    stacked = jnp.concatenate([new_keys, new_values], axis=0)
    out_kv[...] = jnp.dot(weave, stacked, preferred_element_type=jnp.float32).astype(jnp.bfloat16)
    by, of = iota((rows, rows), 0), iota((rows, rows), 1)
    seen = (by % reqs == of % reqs) & (of // reqs <= by // reqs)
    live = table[2]
    for g in range(old.shape[0]):
        span = slice(g * HEAD, (g + 1) * HEAD)
        scores = contract_last(queries[:, span], new_keys) * scale
        scores = jnp.where(seen, scores, -1e30)
        before, old_top, old_total = old[g, :, 0:HEAD], old[g, :, HEAD : HEAD + 1], old[g, :, 2 * HEAD : 2 * HEAD + 1]
        top = jnp.maximum(old_top, jnp.max(scores, axis=-1, keepdims=True))
        shrink = jnp.exp(old_top - top)
        grown = jnp.exp(scores - top)
        total = shrink * old_total + jnp.sum(grown, axis=-1, keepdims=True)
        fresh = (grown / total).astype(jnp.bfloat16)
        mixed = before * (shrink / total) + jnp.dot(
            fresh, new_values, preferred_element_type=jnp.float32
        )
        out_attn[:, span] = (mixed * live).astype(jnp.bfloat16)


def near(x):
    return pltpu.with_memory_space_constraint(x, pltpu.VMEM)


def small(mebibytes):
    return pltpu.CompilerParams(vmem_limit_bytes=mebibytes << 20)


def spread(x, axis, groups=None):
    return lax.all_to_all(x, axis, 0, 0, axis_index_groups=groups)


def local(hidden, norm_gain, w_kv, queries, cache_kv, exits, lengths):
    num_steps, _, local_reqs, width = hidden.shape
    rows = num_steps * local_reqs
    slots = num_steps * EXIT_CAP
    sections = lax.axis_size("section")
    section_index = lax.axis_index("section")
    parts = lax.axis_size("tp")
    chips = parts // 2
    core = lax.axis_index("tp") % 2
    kv_local = w_kv.shape[-1]
    groups = queries.shape[-1] // kv_local
    scale = HEAD ** (-0.5)

    own = hidden.reshape(rows, width)
    flat_exits = exits.reshape(rows)
    section_scalar = section_index.reshape(1)
    outgoing = pl.pallas_call(
        leaving_kernel,
        out_shape=pltpu.VMEM((sections, slots, width), jnp.bfloat16),
        in_specs=[SMEM, VMEM, VMEM],
        out_specs=VMEM,
        compiler_params=small(4),
        name="leaving",
    )(section_scalar, exits, own)
    arrived = spread(outgoing, "section").reshape(sections * slots, width)

    take, kept = pl.pallas_call(
        choose_kernel,
        out_shape=(
            pltpu.VMEM((rows, sections * slots), jnp.bfloat16),
            pltpu.VMEM((rows, width), jnp.bfloat16),
        ),
        in_specs=[SMEM, VMEM, VMEM],
        out_specs=(VMEM, VMEM),
        compiler_params=small(4),
        name="choose",
    )(section_scalar, exits, own)
    step_of = jnp.arange(num_steps, dtype=jnp.int32)[:, None]
    positions = (lengths[None, :] + step_of).reshape(rows)
    exponent = jnp.arange(HEAD // 2, dtype=jnp.float32) * (2.0 / HEAD)
    angles = positions.astype(jnp.float32)[:, None] * ROPE_BASE ** (-exponent)
    cosine, sine = jnp.cos(angles), jnp.sin(angles)
    live = (section_index < flat_exits).astype(jnp.float32)
    table = jnp.stack(
        [
            jnp.concatenate([cosine, cosine], axis=-1),
            jnp.concatenate([-sine, sine], axis=-1),
            jnp.broadcast_to(live[:, None], (rows, HEAD)),
        ]
    )
    by_request = queries.reshape(num_steps, local_reqs, groups, HEAD).transpose(1, 0, 2, 3)
    weight = pl.pallas_call(
        split_kernel,
        grid=(parts,),
        out_shape=pltpu.HBM((parts, width, 2 * HEAD), jnp.bfloat16),
        in_specs=[pl.BlockSpec((2 * width, HEAD), lambda i: (i, 0))],
        out_specs=pl.BlockSpec((1, width, 2 * HEAD), lambda i: (i, 0, 0)),
        compiler_params=small(8),
        name="split",
    )(pltpu.with_memory_space_constraint(w_kv.reshape(2 * D, HEAD), pltpu.HBM))
    old = pl.pallas_call(
        lambda *refs: past_kernel(scale, *refs),
        out_shape=pltpu.VMEM((groups, rows, 3 * HEAD), jnp.float32),
        in_specs=[SMEM, VMEM, VMEM],
        out_specs=VMEM,
        compiler_params=small(8),
        name="past",
    )(lengths, near(by_request.reshape(rows * groups, HEAD)), near(cache_kv[0]))

    weight, old, table, take, kept, arrived = lax.optimization_barrier(
        (weight, old, table, take, kept, arrived)
    )
    sent = pl.pallas_call(
        place_kernel,
        out_shape=pltpu.VMEM((chips, rows + GAIN_ROWS, width), jnp.bfloat16),
        in_specs=[VMEM] * 4,
        out_specs=VMEM,
        compiler_params=small(4),
        name="place",
    )(near(take), near(kept), near(arrived), near(norm_gain))
    same_core = [[2 * x + c for x in range(chips)] for c in range(2)]
    mine = spread(sent, "tp", same_core)
    other = lax.ppermute(mine, "tp", [(i, i ^ 1) for i in range(parts)])

    attended, fresh = pl.pallas_call(
        lambda *refs: finish_kernel(local_reqs, scale, *refs),
        out_shape=(
            jax.ShapeDtypeStruct((rows, groups * HEAD), jnp.bfloat16),
            jax.ShapeDtypeStruct((2 * rows, HEAD), jnp.bfloat16),
        ),
        in_specs=[SMEM, VMEM, VMEM, pl.BlockSpec(memory_space=pltpu.HBM)] + [VMEM] * 3,
        out_specs=(VMEM, VMEM),
        scratch_shapes=[
            pltpu.VMEM((parts, width, 2 * HEAD), jnp.bfloat16),
            pltpu.SemaphoreType.DMA((parts,)),
        ],
        compiler_params=small(24),
        name="finish",
    )(
        core.reshape(1),
        near(mine),
        near(other),
        pltpu.with_memory_space_constraint(weight, pltpu.HBM),
        near(queries.reshape(rows, groups * HEAD)),
        near(old),
        near(table),
    )
    return (
        attended.reshape(num_steps, 1, local_reqs, groups * HEAD),
        fresh.reshape(num_steps, 1, local_reqs, 2, kv_local),
    )


def solution(mesh):
    placed = (
        P(None, "section", "req", "tp"),
        P("section", "tp"),
        P("section", None, None, "tp"),
        P(None, "section", "req", "tp"),
        P("section", "req", None, None, "tp"),
        P(None, "req"),
        P("req"),
    )
    return jax.shard_map(
        local,
        mesh=mesh,
        in_specs=placed,
        out_specs=(P(None, "section", "req", "tp"), P(None, "section", "req", None, "tp")),
        check_vma=False,
    )
```

```python
import jax
import jax.numpy as jnp
from jax import lax
from jax.experimental import pallas as pl
from jax.experimental.pallas import tpu as pltpu
from jax.sharding import PartitionSpec as P

D = 8192
HEAD = 128
EXIT_CAP = 2
EXTRA = 16


EPSILON = 1e-05
ROPE_BASE = 500000.0
VMEM = pl.BlockSpec(memory_space=pltpu.VMEM)
SMEM = pl.BlockSpec(memory_space=pltpu.SMEM)
HBM = pl.BlockSpec(memory_space=pltpu.HBM)


def iota(shape, axis):
    return lax.broadcasted_iota(jnp.int32, shape, axis)


def contract_last(a, b):
    return lax.dot_general(a, b, (((1,), (1,)), ((), ())), preferred_element_type=jnp.float32)


def as_bf16(mask):
    return mask.astype(jnp.float32).astype(jnp.bfloat16)


def exact(a, b):
    return jnp.dot(a, b, preferred_element_type=jnp.float32)


def ranks(same):
    reqs = same.shape[1]
    before = iota((reqs, reqs), 0) < iota((reqs, reqs), 1)
    return exact(as_bf16(same), as_bf16(before))


def leaving_kernel(section, exits_far, own_far, out, exits, own, chosen, sems):
    steps, reqs = exits.shape
    rows = own.shape[0]
    copies = out.shape[0]
    load_exits = pltpu.make_async_copy(exits_far, exits, sems.at[copies])
    load_own = pltpu.make_async_copy(own_far, own, sems.at[copies + 1])
    load_exits.start()
    load_own.start()
    load_exits.wait()
    here = exits[...] == section[0]
    rank = ranks(here)
    picks = [here & (rank == k) for k in range(EXIT_CAP)]
    picks = jnp.concatenate([pick.astype(jnp.float32) for pick in picks], axis=0)
    widen = as_bf16(iota((reqs, rows), 0) == iota((reqs, rows), 1) % reqs)
    wide = exact(picks.astype(jnp.bfloat16), widen)
    slots = EXIT_CAP * steps
    match = iota((slots, rows), 0) % steps == iota((slots, rows), 1) // reqs
    wide = jnp.where(match, wide, 0.0).astype(jnp.bfloat16)
    load_own.wait()
    chosen[...] = exact(wide, own[...]).astype(jnp.bfloat16)
    stores = [pltpu.make_async_copy(chosen, out.at[k], sems.at[k]) for k in range(copies)]
    for store in stores:
        store.start()
    for store in stores:
        store.wait()


def choose_kernel(section, exits, own, take, kept):
    steps, reqs = exits.shape
    rows, reach = take.shape
    slots = EXIT_CAP * steps
    layer = exits[...]
    rank = jnp.zeros((steps, reqs), jnp.float32)
    for e in range(reach // slots):
        same = layer == e
        rank = jnp.where(same, ranks(same), rank)
    gone = layer < section[0]
    slot = layer * slots + rank.astype(jnp.int32) * steps + iota((steps, reqs), 0)
    slot = jnp.where(gone, slot, -1).astype(jnp.float32)
    spread_steps = as_bf16(iota((rows, steps), 0) // reqs == iota((rows, steps), 1))
    column = exact(spread_steps, slot.astype(jnp.bfloat16))
    own_lane = iota((rows, reqs), 0) % reqs == iota((rows, reqs), 1)
    column = jnp.sum(jnp.where(own_lane, column, 0.0), axis=-1, keepdims=True)
    take[...] = as_bf16(column.astype(jnp.int32) == iota((rows, reach), 1))
    kept[...] = jnp.where(column >= 0.0, 0.0, own[...].astype(jnp.float32)).astype(jnp.bfloat16)


def split_kernel(weight, out):
    half = 128
    to, fro = iota((2 * half, 2 * half), 0), iota((2 * half, 2 * half), 1)
    split = as_bf16(fro == jnp.where(to < half, 2 * to, 2 * (to - half) + 1))
    for j in range(weight.shape[0] // (2 * half)):
        pair = exact(split, weight[2 * half * j : 2 * half * (j + 1), :]).astype(jnp.bfloat16)
        out[0, half * j : half * (j + 1), 0:HEAD] = pair[:half]
        out[0, half * j : half * (j + 1), HEAD : 2 * HEAD] = pair[half:]


def past_kernel(scale, lengths, queries, cache, out):
    reqs = cache.shape[0]
    per = queries.shape[0] // reqs
    groups = out.shape[0]
    for r in range(reqs):
        scores = contract_last(queries[r * per : (r + 1) * per, :], cache[r, 0]) * scale
        scores = jnp.where(iota(scores.shape, 1) < lengths[r], scores, -1e30)
        top = jnp.max(scores, axis=-1, keepdims=True)
        grown = jnp.exp(scores - top)
        total = jnp.sum(grown, axis=-1, keepdims=True)
        high = grown.astype(jnp.bfloat16)
        low = (grown - high.astype(jnp.float32)).astype(jnp.bfloat16)
        mixed = exact(high, cache[r, 1]) + exact(low, cache[r, 1])
        top = jnp.broadcast_to(top, (per, HEAD))
        total = jnp.broadcast_to(total, (per, HEAD))
        for t in range(per // groups):
            row = slice(t * reqs + r, t * reqs + r + 1)
            for g in range(groups):
                at = slice(t * groups + g, t * groups + g + 1)
                out[g, row, 0:HEAD] = mixed[at]
                out[g, row, HEAD : 2 * HEAD] = top[at]
                out[g, row, 2 * HEAD : 3 * HEAD] = total[at]


def diagonal(rows):
    return iota((rows, HEAD), 0) == iota((rows, HEAD), 1)


def place_kernel(take, kept, arrived, gain, out):
    rows, width = kept.shape
    blocks = width // HEAD
    source = exact(take[...], arrived[...])
    source = (source + kept[...].astype(jnp.float32)).astype(jnp.bfloat16)
    values = source.astype(jnp.float32)
    squares = jnp.zeros((rows, HEAD), jnp.float32)
    for j in range(blocks):
        value = values[:, HEAD * j : HEAD * (j + 1)]
        squares = squares + value * value
    squares = jnp.sum(squares, axis=-1, keepdims=True)
    squares = jnp.sum(jnp.where(diagonal(rows), squares, 0.0), axis=0, keepdims=True)
    high = squares.astype(jnp.bfloat16).astype(jnp.float32)
    middle = (squares - high).astype(jnp.bfloat16).astype(jnp.float32)
    low = squares - high - middle
    at = iota((8, HEAD), 0)
    sums = jnp.zeros((8, HEAD), jnp.float32)
    for k, piece in enumerate((high, middle, low)):
        sums = jnp.where(at == k, piece, sums)
    gains = jnp.zeros((8, HEAD), jnp.float32)
    for j in range(blocks):
        gains = jnp.where(at == j, gain[:, HEAD * j : HEAD * (j + 1)].astype(jnp.float32), gains)
    extra = jnp.concatenate([gains, sums], axis=0).astype(jnp.bfloat16)
    for k in range(out.shape[0]):
        for j in range(blocks):
            out[k, rows * j : rows * (j + 1), :] = source[:, HEAD * j : HEAD * (j + 1)]
        out[k, rows * blocks : rows * blocks + EXTRA, :] = extra


def finish_kernel(
    reqs, scale, core, mine, other, weight, queries, old, table, out_attn, out_kv, held_weight, sems
):
    rows = queries.shape[0]
    chips = mine.shape[0]
    blocks = weight.shape[1] // HEAD
    order = [(mine, x, 2 * x + core[0]) for x in range(chips)]
    order += [(other, x, 2 * x + 1 - core[0]) for x in range(chips)]
    loads = [
        pltpu.make_async_copy(weight.at[part], held_weight.at[i], sems.at[i])
        for i, (_, _, part) in enumerate(order)
    ]
    for load in loads:
        load.start()
    squares = jnp.zeros((8, HEAD), jnp.float32)
    extras = []
    for held, x, _ in order:
        extra = held[x, rows * blocks : rows * blocks + EXTRA, :].astype(jnp.float32)
        extras.append(extra[:8])
        squares = squares + extra[8:]
    squares = jnp.sum(squares, axis=0, keepdims=True)
    squares = jnp.sum(jnp.where(diagonal(rows), squares, 0.0), axis=-1, keepdims=True)
    inverse = lax.rsqrt(squares / D + EPSILON)
    pairs = jnp.zeros((rows, 2 * HEAD), jnp.float32)
    for i, (held, x, _) in enumerate(order):
        normed = []
        for j in range(blocks):
            value = held[x, rows * j : rows * (j + 1), :].astype(jnp.float32)
            normed.append((value * inverse * extras[i][j : j + 1]).astype(jnp.bfloat16))
        loads[i].wait()
        pairs = pairs + exact(jnp.concatenate(normed, axis=1), held_weight[i])
    keys = pairs[:, :HEAD]
    turned = pltpu.roll(keys, HEAD // 2, 1)
    new_keys = (keys * table[0] + turned * table[1]).astype(jnp.bfloat16)
    new_values = pairs[:, HEAD:].astype(jnp.bfloat16)
    padding = jnp.zeros((HEAD - rows, HEAD), jnp.bfloat16)
    wide_keys = jnp.concatenate([new_keys, padding], axis=0)
    wide_values = jnp.concatenate([new_values, padding], axis=0)
    by, of = iota((rows, HEAD), 0), iota((rows, HEAD), 1)
    seen = (by % reqs == of % reqs) & (of // reqs <= by // reqs)
    live = table[2]
    for g in range(old.shape[0]):
        span = slice(g * HEAD, (g + 1) * HEAD)
        scores = contract_last(queries[:, span], wide_keys) * scale
        scores = jnp.where(seen, scores, -1e30)
        old_top = old[g, :, HEAD : 2 * HEAD]
        top = jnp.maximum(old_top, jnp.max(scores, axis=-1, keepdims=True))
        shrink = jnp.exp(old_top - top)
        grown = jnp.exp(scores - top)
        total = shrink * old[g, :, 2 * HEAD :] + jnp.sum(grown, axis=-1, keepdims=True)
        part = 1.0 / total
        fresh = (grown * part).astype(jnp.bfloat16)
        mixed = old[g, :, 0:HEAD] * (shrink * part) + exact(fresh, wide_values)
        out_attn[:, span] = (mixed * live).astype(jnp.bfloat16)
    to, fro = iota((2 * rows, 2 * rows), 0), iota((2 * rows, 2 * rows), 1)
    weave = as_bf16(fro == (to // 2) + rows * (to % 2))
    stacked = jnp.concatenate([new_keys, new_values], axis=0)
    out_kv[...] = exact(weave, stacked).astype(jnp.bfloat16)


def far(x):
    return pltpu.with_memory_space_constraint(x, pltpu.HBM)


def near(x):
    return pltpu.with_memory_space_constraint(x, pltpu.VMEM)


def small(mebibytes):
    return pltpu.CompilerParams(vmem_limit_bytes=mebibytes << 20)


def spread(x, axis, groups=None):
    return lax.all_to_all(x, axis, 0, 0, axis_index_groups=groups)


def local(hidden, norm_gain, w_kv, queries, cache_kv, exits, lengths):
    num_steps, _, local_reqs, width = hidden.shape
    rows = num_steps * local_reqs
    slots = num_steps * EXIT_CAP
    sections = lax.axis_size("section")
    section_index = lax.axis_index("section")
    parts = lax.axis_size("tp")
    chips = parts // 2
    core = lax.axis_index("tp") % 2
    kv_local = w_kv.shape[-1]
    groups = queries.shape[-1] // kv_local
    scale = HEAD ** (-0.5)

    own = hidden.reshape(rows, width)
    flat_exits = exits.reshape(rows)
    section_scalar = section_index.reshape(1)
    outgoing = pl.pallas_call(
        leaving_kernel,
        out_shape=pltpu.HBM((sections, slots, width), jnp.bfloat16),
        in_specs=[SMEM, HBM, HBM],
        out_specs=HBM,
        scratch_shapes=[
            pltpu.VMEM(exits.shape, jnp.int32),
            pltpu.VMEM(own.shape, jnp.bfloat16),
            pltpu.VMEM((slots, width), jnp.bfloat16),
            pltpu.SemaphoreType.DMA((sections + 2,)),
        ],
        compiler_params=small(4),
        name="leaving",
    )(section_scalar, far(exits), far(own))
    arrived = spread(outgoing, "section").reshape(sections * slots, width)

    take, kept = pl.pallas_call(
        choose_kernel,
        out_shape=(
            pltpu.VMEM((rows, sections * slots), jnp.bfloat16),
            pltpu.VMEM((rows, width), jnp.bfloat16),
        ),
        in_specs=[SMEM, VMEM, VMEM],
        out_specs=(VMEM, VMEM),
        compiler_params=small(4),
        name="choose",
    )(section_scalar, exits, own)
    step_of = jnp.arange(num_steps, dtype=jnp.int32)[:, None]
    positions = (lengths[None, :] + step_of).reshape(rows)
    exponent = jnp.arange(HEAD // 2, dtype=jnp.float32) * (2.0 / HEAD)
    angles = positions.astype(jnp.float32)[:, None] * ROPE_BASE ** (-exponent)
    cosine, sine = jnp.cos(angles), jnp.sin(angles)
    live = (section_index < flat_exits).astype(jnp.float32)
    table = jnp.stack(
        [
            jnp.concatenate([cosine, cosine], axis=-1),
            jnp.concatenate([-sine, sine], axis=-1),
            jnp.broadcast_to(live[:, None], (rows, HEAD)),
        ]
    )
    by_request = queries.reshape(num_steps, local_reqs, groups, HEAD).transpose(1, 0, 2, 3)
    weight = pl.pallas_call(
        split_kernel,
        grid=(parts,),
        out_shape=pltpu.HBM((parts, width, 2 * HEAD), jnp.bfloat16),
        in_specs=[pl.BlockSpec((2 * width, HEAD), lambda i: (i, 0))],
        out_specs=pl.BlockSpec((1, width, 2 * HEAD), lambda i: (i, 0, 0)),
        compiler_params=small(8),
        name="split",
    )(far(w_kv.reshape(2 * D, HEAD)))
    old = pl.pallas_call(
        lambda *refs: past_kernel(scale, *refs),
        out_shape=pltpu.VMEM((groups, rows, 3 * HEAD), jnp.float32),
        in_specs=[SMEM, VMEM, VMEM],
        out_specs=VMEM,
        compiler_params=small(8),
        name="past",
    )(lengths, near(by_request.reshape(rows * groups, HEAD)), near(cache_kv[0]))

    weight, old, table, take, kept, arrived = lax.optimization_barrier(
        (weight, old, table, take, kept, arrived)
    )
    sent = pl.pallas_call(
        place_kernel,
        out_shape=pltpu.VMEM((chips, rows * (width // HEAD) + EXTRA, HEAD), jnp.bfloat16),
        in_specs=[VMEM] * 4,
        out_specs=VMEM,
        compiler_params=small(4),
        name="place",
    )(near(take), near(kept), near(arrived), near(norm_gain))
    same_core = [[2 * x + c for x in range(chips)] for c in range(2)]
    mine = spread(sent, "tp", same_core)
    other = lax.ppermute(mine, "tp", [(i, i ^ 1) for i in range(parts)])

    attended, fresh = pl.pallas_call(
        lambda *refs: finish_kernel(local_reqs, scale, *refs),
        out_shape=(
            jax.ShapeDtypeStruct((rows, groups * HEAD), jnp.bfloat16),
            jax.ShapeDtypeStruct((2 * rows, HEAD), jnp.bfloat16),
        ),
        in_specs=[SMEM, VMEM, VMEM, HBM] + [VMEM] * 3,
        out_specs=(VMEM, VMEM),
        scratch_shapes=[
            pltpu.VMEM((parts, width, 2 * HEAD), jnp.bfloat16),
            pltpu.SemaphoreType.DMA((parts,)),
        ],
        compiler_params=small(24),
        name="finish",
    )(
        core.reshape(1),
        near(mine),
        near(other),
        far(weight),
        near(queries.reshape(rows, groups * HEAD)),
        near(old),
        near(table),
    )
    return (
        attended.reshape(num_steps, 1, local_reqs, groups * HEAD),
        fresh.reshape(num_steps, 1, local_reqs, 2, kv_local),
    )


def solution(mesh):
    placed = (
        P(None, "section", "req", "tp"),
        P("section", "tp"),
        P("section", None, None, "tp"),
        P(None, "section", "req", "tp"),
        P("section", "req", None, None, "tp"),
        P(None, "req"),
        P("req"),
    )
    return jax.shard_map(
        local,
        mesh=mesh,
        in_specs=placed,
        out_specs=(P(None, "section", "req", "tp"), P(None, "section", "req", None, "tp")),
        check_vma=False,
    )
```

```python
import jax
import jax.numpy as jnp
from jax import lax
from jax.experimental import pallas as pl
from jax.experimental.pallas import tpu as pltpu
from jax.sharding import PartitionSpec as P

D = 8192
HEAD = 128
EXIT_CAP = 2
EXTRA = 8


EPSILON = 1e-05
ROPE_BASE = 500000.0
VMEM = pl.BlockSpec(memory_space=pltpu.VMEM)
SMEM = pl.BlockSpec(memory_space=pltpu.SMEM)
HBM = pl.BlockSpec(memory_space=pltpu.HBM)


def iota(shape, axis):
    return lax.broadcasted_iota(jnp.int32, shape, axis)


def contract_last(a, b):
    return lax.dot_general(a, b, (((1,), (1,)), ((), ())), preferred_element_type=jnp.float32)


def as_bf16(mask):
    return mask.astype(jnp.float32).astype(jnp.bfloat16)


def exact(a, b):
    return jnp.dot(a, b, preferred_element_type=jnp.float32)


def ranks(same):
    reqs = same.shape[1]
    before = iota((reqs, reqs), 0) < iota((reqs, reqs), 1)
    return exact(as_bf16(same), as_bf16(before))


def leaving_kernel(section, exits_far, own_far, out, exits, own, chosen, sems):
    steps, reqs = exits.shape
    rows = own.shape[0]
    copies = out.shape[0]
    load_exits = pltpu.make_async_copy(exits_far, exits, sems.at[copies])
    load_own = pltpu.make_async_copy(own_far, own, sems.at[copies + 1])
    load_exits.start()
    load_own.start()
    load_exits.wait()
    here = exits[...] == section[0]
    rank = ranks(here)
    picks = [here & (rank == k) for k in range(EXIT_CAP)]
    picks = jnp.concatenate([pick.astype(jnp.float32) for pick in picks], axis=0)
    widen = as_bf16(iota((reqs, rows), 0) == iota((reqs, rows), 1) % reqs)
    wide = exact(picks.astype(jnp.bfloat16), widen)
    slots = EXIT_CAP * steps
    match = iota((slots, rows), 0) % steps == iota((slots, rows), 1) // reqs
    wide = jnp.where(match, wide, 0.0).astype(jnp.bfloat16)
    load_own.wait()
    chosen[...] = exact(wide, own[...]).astype(jnp.bfloat16)
    stores = [pltpu.make_async_copy(chosen, out.at[k], sems.at[k]) for k in range(copies)]
    for store in stores:
        store.start()
    for store in stores:
        store.wait()


def choose_kernel(section, exits, own, take, kept):
    steps, reqs = exits.shape
    rows, reach = take.shape
    slots = EXIT_CAP * steps
    layer = exits[...]
    rank = jnp.zeros((steps, reqs), jnp.float32)
    for e in range(reach // slots):
        same = layer == e
        rank = jnp.where(same, ranks(same), rank)
    gone = layer < section[0]
    slot = layer * slots + rank.astype(jnp.int32) * steps + iota((steps, reqs), 0)
    slot = jnp.where(gone, slot, -1).astype(jnp.float32)
    spread_steps = as_bf16(iota((rows, steps), 0) // reqs == iota((rows, steps), 1))
    column = exact(spread_steps, slot.astype(jnp.bfloat16))
    own_lane = iota((rows, reqs), 0) % reqs == iota((rows, reqs), 1)
    column = jnp.sum(jnp.where(own_lane, column, 0.0), axis=-1, keepdims=True)
    take[...] = as_bf16(column.astype(jnp.int32) == iota((rows, reach), 1))
    kept[...] = jnp.where(column >= 0.0, 0.0, own[...].astype(jnp.float32)).astype(jnp.bfloat16)


def split_kernel(weight, out, wide):
    rows = weight.shape[0] // 2
    wide[...] = weight[...].astype(jnp.float32)
    for k in range(2):
        half = wide[pl.ds(k, rows, stride=2), :].astype(jnp.bfloat16)
        for p in range(out.shape[0]):
            part = half[p * out.shape[1] : (p + 1) * out.shape[1]]
            out[p, :, HEAD * k : HEAD * (k + 1)] = part


def past_kernel(scale, lengths, queries, cache, out):
    reqs = cache.shape[0]
    per = queries.shape[0] // reqs
    groups = out.shape[0]
    for r in range(reqs):
        scores = contract_last(queries[r * per : (r + 1) * per, :], cache[r, 0]) * scale
        scores = jnp.where(iota(scores.shape, 1) < lengths[r], scores, -1e30)
        top = jnp.max(scores, axis=-1, keepdims=True)
        grown = jnp.exp(scores - top)
        total = jnp.sum(grown, axis=-1, keepdims=True)
        high = grown.astype(jnp.bfloat16)
        low = (grown - high.astype(jnp.float32)).astype(jnp.bfloat16)
        mixed = exact(high, cache[r, 1]) + exact(low, cache[r, 1])
        top = jnp.broadcast_to(top, (per, HEAD))
        total = jnp.broadcast_to(total, (per, HEAD))
        for t in range(per // groups):
            row = slice(t * reqs + r, t * reqs + r + 1)
            for g in range(groups):
                at = slice(t * groups + g, t * groups + g + 1)
                out[g, row, 0:HEAD] = mixed[at]
                out[g, row, HEAD : 2 * HEAD] = top[at]
                out[g, row, 2 * HEAD : 3 * HEAD] = total[at]


def diagonal(rows):
    return iota((rows, HEAD), 0) == iota((rows, HEAD), 1)


def place_kernel(take, kept, arrived, gain, out):
    rows, width = kept.shape
    blocks = width // HEAD
    source = exact(take[...], arrived[...])
    source = (source + kept[...].astype(jnp.float32)).astype(jnp.bfloat16)
    values = source.astype(jnp.float32)
    squares = jnp.zeros((rows, HEAD), jnp.float32)
    for j in range(blocks):
        value = values[:, HEAD * j : HEAD * (j + 1)]
        squares = squares + value * value
    squares = jnp.sum(squares, axis=-1, keepdims=True)
    squares = jnp.sum(jnp.where(diagonal(rows), squares, 0.0), axis=0, keepdims=True)
    high = squares.astype(jnp.bfloat16).astype(jnp.float32)
    middle = (squares - high).astype(jnp.bfloat16).astype(jnp.float32)
    low = squares - high - middle
    at = iota((EXTRA, HEAD), 0)
    sums = jnp.zeros((EXTRA, HEAD), jnp.float32)
    for k, piece in enumerate((high, middle, low)):
        sums = jnp.where(at == k, piece, sums)
    scaled = (values * gain[...].astype(jnp.float32)).astype(jnp.bfloat16)
    extra = sums.astype(jnp.bfloat16)
    for k in range(out.shape[0]):
        for j in range(blocks):
            out[k, rows * j : rows * (j + 1), :] = scaled[:, HEAD * j : HEAD * (j + 1)]
        out[k, rows * blocks : rows * blocks + EXTRA, :] = extra


def gathered(held, x, rows, blocks):
    return jnp.concatenate([held[x, rows * j : rows * (j + 1), :] for j in range(blocks)], axis=1)


def half_kernel(core, held, weight, pairs, ahead, mine, sems):
    chips = held.shape[0]
    blocks = weight.shape[1] // HEAD
    rows = pairs.shape[0]
    loads = [pltpu.make_async_copy(weight.at[2 * x + core[0]], mine.at[x], sems.at[x]) for x in range(chips)]
    more = [
        pltpu.make_async_copy(weight.at[2 * x + 1 - core[0]], ahead.at[x], sems.at[chips + x])
        for x in range(chips)
    ]
    for load in loads + more:
        load.start()
    total = jnp.zeros(pairs.shape, jnp.float32)
    for x in range(chips):
        loads[x].wait()
        total = total + exact(gathered(held, x, rows, blocks), mine[x])
    pairs[...] = total
    for load in more:
        load.wait()


def finish_kernel(reqs, scale, mine, other, pairs, weight, queries, old, table, out_attn, out_kv):
    rows = queries.shape[0]
    chips = mine.shape[0]
    blocks = weight.shape[1] // HEAD
    squares = jnp.zeros((EXTRA, HEAD), jnp.float32)
    for held in (mine, other):
        for x in range(chips):
            squares = squares + held[x, rows * blocks : rows * blocks + EXTRA, :].astype(jnp.float32)
    squares = jnp.sum(squares, axis=0, keepdims=True)
    squares = jnp.sum(jnp.where(diagonal(rows), squares, 0.0), axis=-1, keepdims=True)
    inverse = lax.rsqrt(squares / D + EPSILON)
    pairs = pairs[...]
    for x in range(chips):
        pairs = pairs + exact(gathered(other, x, rows, blocks), weight[x])
    pairs = pairs * inverse
    keys = pairs[:, :HEAD]
    turned = pltpu.roll(keys, HEAD // 2, 1)
    new_keys = (keys * table[0] + turned * table[1]).astype(jnp.bfloat16)
    new_values = pairs[:, HEAD:].astype(jnp.bfloat16)
    padding = jnp.zeros((HEAD - rows, HEAD), jnp.bfloat16)
    wide_keys = jnp.concatenate([new_keys, padding], axis=0)
    wide_values = jnp.concatenate([new_values, padding], axis=0)
    by, of = iota((rows, HEAD), 0), iota((rows, HEAD), 1)
    seen = (by % reqs == of % reqs) & (of // reqs <= by // reqs)
    live = table[2]
    for g in range(old.shape[0]):
        span = slice(g * HEAD, (g + 1) * HEAD)
        scores = contract_last(queries[:, span], wide_keys) * scale
        scores = jnp.where(seen, scores, -1e30)
        old_top = old[g, :, HEAD : 2 * HEAD]
        top = jnp.maximum(old_top, jnp.max(scores, axis=-1, keepdims=True))
        shrink = jnp.exp(old_top - top)
        grown = jnp.exp(scores - top)
        total = shrink * old[g, :, 2 * HEAD :] + jnp.sum(grown, axis=-1, keepdims=True)
        part = 1.0 / total
        fresh = (grown * part).astype(jnp.bfloat16)
        mixed = old[g, :, 0:HEAD] * (shrink * part) + exact(fresh, wide_values)
        out_attn[:, span] = (mixed * live).astype(jnp.bfloat16)
    to, fro = iota((2 * rows, 2 * rows), 0), iota((2 * rows, 2 * rows), 1)
    weave = as_bf16(fro == (to // 2) + rows * (to % 2))
    stacked = jnp.concatenate([new_keys, new_values], axis=0)
    out_kv[...] = exact(weave, stacked).astype(jnp.bfloat16)


def far(x):
    return pltpu.with_memory_space_constraint(x, pltpu.HBM)


def near(x):
    return pltpu.with_memory_space_constraint(x, pltpu.VMEM)


def small(mebibytes):
    return pltpu.CompilerParams(vmem_limit_bytes=mebibytes << 20)


def spread(x, axis, groups=None):
    return lax.all_to_all(x, axis, 0, 0, axis_index_groups=groups)


def local(hidden, norm_gain, w_kv, queries, cache_kv, exits, lengths):
    num_steps, _, local_reqs, width = hidden.shape
    rows = num_steps * local_reqs
    slots = num_steps * EXIT_CAP
    sections = lax.axis_size("section")
    section_index = lax.axis_index("section")
    parts = lax.axis_size("tp")
    chips = parts // 2
    core = lax.axis_index("tp") % 2
    kv_local = w_kv.shape[-1]
    groups = queries.shape[-1] // kv_local
    scale = HEAD ** (-0.5)

    own = hidden.reshape(rows, width)
    flat_exits = exits.reshape(rows)
    section_scalar = section_index.reshape(1)
    outgoing = pl.pallas_call(
        leaving_kernel,
        out_shape=pltpu.HBM((sections, slots, width), jnp.bfloat16),
        in_specs=[SMEM, HBM, HBM],
        out_specs=HBM,
        scratch_shapes=[
            pltpu.VMEM(exits.shape, jnp.int32),
            pltpu.VMEM(own.shape, jnp.bfloat16),
            pltpu.VMEM((slots, width), jnp.bfloat16),
            pltpu.SemaphoreType.DMA((sections + 2,)),
        ],
        compiler_params=small(4),
        name="leaving",
    )(section_scalar, far(exits), far(own))
    arrived = spread(outgoing, "section").reshape(sections * slots, width)

    take, kept = pl.pallas_call(
        choose_kernel,
        out_shape=(
            pltpu.VMEM((rows, sections * slots), jnp.bfloat16),
            pltpu.VMEM((rows, width), jnp.bfloat16),
        ),
        in_specs=[SMEM, VMEM, VMEM],
        out_specs=(VMEM, VMEM),
        compiler_params=small(4),
        name="choose",
    )(section_scalar, exits, own)
    step_of = jnp.arange(num_steps, dtype=jnp.int32)[:, None]
    positions = (lengths[None, :] + step_of).reshape(rows)
    exponent = jnp.arange(HEAD // 2, dtype=jnp.float32) * (2.0 / HEAD)
    angles = positions.astype(jnp.float32)[:, None] * ROPE_BASE ** (-exponent)
    cosine, sine = jnp.cos(angles), jnp.sin(angles)
    live = (section_index < flat_exits).astype(jnp.float32)
    table = jnp.stack(
        [
            jnp.concatenate([cosine, cosine], axis=-1),
            jnp.concatenate([-sine, sine], axis=-1),
            jnp.broadcast_to(live[:, None], (rows, HEAD)),
        ]
    )
    by_request = queries.reshape(num_steps, local_reqs, groups, HEAD).transpose(1, 0, 2, 3)
    weight = pl.pallas_call(
        split_kernel,
        grid=(chips,),
        out_shape=pltpu.HBM((parts, width, 2 * HEAD), jnp.bfloat16),
        in_specs=[pl.BlockSpec((4 * width, HEAD), lambda i: (i, 0))],
        out_specs=pl.BlockSpec((2, width, 2 * HEAD), lambda i: (i, 0, 0)),
        scratch_shapes=[pltpu.VMEM((4 * width, HEAD), jnp.float32)],
        compiler_params=small(16),
        name="split",
    )(far(w_kv.reshape(2 * D, HEAD)))
    old = pl.pallas_call(
        lambda *refs: past_kernel(scale, *refs),
        out_shape=pltpu.VMEM((groups, rows, 3 * HEAD), jnp.float32),
        in_specs=[SMEM, VMEM, VMEM],
        out_specs=VMEM,
        compiler_params=small(8),
        name="past",
    )(lengths, near(by_request.reshape(rows * groups, HEAD)), near(cache_kv[0]))

    weight, old, table, take, kept, arrived = lax.optimization_barrier(
        (weight, old, table, take, kept, arrived)
    )
    sent = pl.pallas_call(
        place_kernel,
        out_shape=pltpu.VMEM((chips, rows * (width // HEAD) + EXTRA, HEAD), jnp.bfloat16),
        in_specs=[VMEM] * 4,
        out_specs=VMEM,
        compiler_params=small(4),
        name="place",
    )(near(take), near(kept), near(arrived), near(norm_gain))
    same_core = [[2 * x + c for x in range(chips)] for c in range(2)]
    mine = spread(sent, "tp", same_core)
    other = lax.ppermute(mine, "tp", [(i, i ^ 1) for i in range(parts)])

    pairs, ahead = pl.pallas_call(
        half_kernel,
        out_shape=(
            pltpu.VMEM((rows, 2 * HEAD), jnp.float32),
            pltpu.VMEM((chips, width, 2 * HEAD), jnp.bfloat16),
        ),
        in_specs=[SMEM, VMEM, HBM],
        out_specs=(VMEM, VMEM),
        scratch_shapes=[
            pltpu.VMEM((chips, width, 2 * HEAD), jnp.bfloat16),
            pltpu.SemaphoreType.DMA((parts,)),
        ],
        compiler_params=small(16),
        name="half",
    )(core.reshape(1), near(mine), far(weight))
    attended, fresh = pl.pallas_call(
        lambda *refs: finish_kernel(local_reqs, scale, *refs),
        out_shape=(
            jax.ShapeDtypeStruct((rows, groups * HEAD), jnp.bfloat16),
            jax.ShapeDtypeStruct((2 * rows, HEAD), jnp.bfloat16),
        ),
        in_specs=[VMEM] * 7,
        out_specs=(VMEM, VMEM),
        compiler_params=small(16),
        name="finish",
    )(
        near(mine),
        near(other),
        near(pairs),
        near(ahead),
        near(queries.reshape(rows, groups * HEAD)),
        near(old),
        near(table),
    )
    return (
        attended.reshape(num_steps, 1, local_reqs, groups * HEAD),
        fresh.reshape(num_steps, 1, local_reqs, 2, kv_local),
    )


def solution(mesh):
    placed = (
        P(None, "section", "req", "tp"),
        P("section", "tp"),
        P("section", None, None, "tp"),
        P(None, "section", "req", "tp"),
        P("section", "req", None, None, "tp"),
        P(None, "req"),
        P("req"),
    )
    return jax.shard_map(
        local,
        mesh=mesh,
        in_specs=placed,
        out_specs=(P(None, "section", "req", "tp"), P(None, "section", "req", None, "tp")),
        check_vma=False,
    )
```

```python
import jax
import jax.numpy as jnp
from jax import lax
from jax.experimental import pallas as pl
from jax.experimental.pallas import tpu as pltpu
from jax.sharding import PartitionSpec as P

D = 8192
HEAD = 128
EXIT_CAP = 2
EXTRA = 8


EPSILON = 1e-05
ROPE_BASE = 500000.0
VMEM = pl.BlockSpec(memory_space=pltpu.VMEM)
SMEM = pl.BlockSpec(memory_space=pltpu.SMEM)
HBM = pl.BlockSpec(memory_space=pltpu.HBM)


def iota(shape, axis):
    return lax.broadcasted_iota(jnp.int32, shape, axis)


def contract_last(a, b):
    return lax.dot_general(a, b, (((1,), (1,)), ((), ())), preferred_element_type=jnp.float32)


def as_bf16(mask):
    return mask.astype(jnp.float32).astype(jnp.bfloat16)


def exact(a, b):
    return jnp.dot(a, b, preferred_element_type=jnp.float32)


def ranks(same):
    reqs = same.shape[1]
    before = iota((reqs, reqs), 0) < iota((reqs, reqs), 1)
    return exact(as_bf16(same), as_bf16(before))


def leaving_kernel(section, exits_far, own_far, out, exits, own, chosen, sems):
    steps, reqs = exits.shape
    rows = own.shape[0]
    copies = out.shape[0]
    load_exits = pltpu.make_async_copy(exits_far, exits, sems.at[copies])
    load_own = pltpu.make_async_copy(own_far, own, sems.at[copies + 1])
    load_exits.start()
    load_own.start()
    load_exits.wait()
    here = exits[...] == section[0]
    rank = ranks(here)
    picks = [here & (rank == k) for k in range(EXIT_CAP)]
    picks = jnp.concatenate([pick.astype(jnp.float32) for pick in picks], axis=0)
    widen = as_bf16(iota((reqs, rows), 0) == iota((reqs, rows), 1) % reqs)
    wide = exact(picks.astype(jnp.bfloat16), widen)
    slots = EXIT_CAP * steps
    match = iota((slots, rows), 0) % steps == iota((slots, rows), 1) // reqs
    wide = jnp.where(match, wide, 0.0).astype(jnp.bfloat16)
    load_own.wait()
    chosen[...] = exact(wide, own[...]).astype(jnp.bfloat16)
    stores = [pltpu.make_async_copy(chosen, out.at[k], sems.at[k]) for k in range(copies)]
    for store in stores:
        store.start()
    for store in stores:
        store.wait()


def choose_kernel(section, exits, own, take, kept):
    steps, reqs = exits.shape
    rows, reach = take.shape
    slots = EXIT_CAP * steps
    layer = exits[...]
    rank = jnp.zeros((steps, reqs), jnp.float32)
    for e in range(reach // slots):
        same = layer == e
        rank = jnp.where(same, ranks(same), rank)
    gone = layer < section[0]
    slot = layer * slots + rank.astype(jnp.int32) * steps + iota((steps, reqs), 0)
    slot = jnp.where(gone, slot, -1).astype(jnp.float32)
    spread_steps = as_bf16(iota((rows, steps), 0) // reqs == iota((rows, steps), 1))
    column = exact(spread_steps, slot.astype(jnp.bfloat16))
    own_lane = iota((rows, reqs), 0) % reqs == iota((rows, reqs), 1)
    column = jnp.sum(jnp.where(own_lane, column, 0.0), axis=-1, keepdims=True)
    take[...] = as_bf16(column.astype(jnp.int32) == iota((rows, reach), 1))
    kept[...] = jnp.where(column >= 0.0, 0.0, own[...].astype(jnp.float32)).astype(jnp.bfloat16)


def split_kernel(weight, out, wide):
    rows = weight.shape[0] // 2
    wide[...] = weight[...].astype(jnp.float32)
    for k in range(2):
        half = wide[pl.ds(k, rows, stride=2), :].astype(jnp.bfloat16)
        for p in range(out.shape[0]):
            part = half[p * out.shape[1] : (p + 1) * out.shape[1]]
            out[p, :, HEAD * k : HEAD * (k + 1)] = part


def past_kernel(scale, lengths, queries, cache, out):
    reqs = cache.shape[0]
    per = queries.shape[0] // reqs
    groups = out.shape[0]
    for r in range(reqs):
        scores = contract_last(queries[r * per : (r + 1) * per, :], cache[r, 0]) * scale
        scores = jnp.where(iota(scores.shape, 1) < lengths[r], scores, -1e30)
        top = jnp.max(scores, axis=-1, keepdims=True)
        grown = jnp.exp(scores - top)
        total = jnp.sum(grown, axis=-1, keepdims=True)
        high = grown.astype(jnp.bfloat16)
        low = (grown - high.astype(jnp.float32)).astype(jnp.bfloat16)
        mixed = exact(high, cache[r, 1]) + exact(low, cache[r, 1])
        top = jnp.broadcast_to(top, (per, HEAD))
        total = jnp.broadcast_to(total, (per, HEAD))
        for t in range(per // groups):
            row = slice(t * reqs + r, t * reqs + r + 1)
            for g in range(groups):
                at = slice(t * groups + g, t * groups + g + 1)
                out[g, row, 0:HEAD] = mixed[at]
                out[g, row, HEAD : 2 * HEAD] = top[at]
                out[g, row, 2 * HEAD : 3 * HEAD] = total[at]


def diagonal(rows):
    return iota((rows, HEAD), 0) == iota((rows, HEAD), 1)


def place_kernel(take, kept, arrived, gain, out):
    rows, width = kept.shape
    blocks = width // HEAD
    source = exact(take[...], arrived[...])
    source = (source + kept[...].astype(jnp.float32)).astype(jnp.bfloat16)
    values = source.astype(jnp.float32)
    squares = jnp.zeros((rows, HEAD), jnp.float32)
    for j in range(blocks):
        value = values[:, HEAD * j : HEAD * (j + 1)]
        squares = squares + value * value
    squares = jnp.sum(squares, axis=-1, keepdims=True)
    squares = jnp.sum(jnp.where(diagonal(rows), squares, 0.0), axis=0, keepdims=True)
    high = squares.astype(jnp.bfloat16).astype(jnp.float32)
    middle = (squares - high).astype(jnp.bfloat16).astype(jnp.float32)
    low = squares - high - middle
    at = iota((EXTRA, HEAD), 0)
    sums = jnp.zeros((EXTRA, HEAD), jnp.float32)
    for k, piece in enumerate((high, middle, low)):
        sums = jnp.where(at == k, piece, sums)
    scaled = (values * gain[...].astype(jnp.float32)).astype(jnp.bfloat16)
    extra = sums.astype(jnp.bfloat16)
    for k in range(out.shape[0]):
        for j in range(blocks):
            out[k, rows * j : rows * (j + 1), :] = scaled[:, HEAD * j : HEAD * (j + 1)]
        out[k, rows * blocks : rows * blocks + EXTRA, :] = extra


def gathered(held, x, rows, blocks):
    return jnp.concatenate([held[x, rows * j : rows * (j + 1), :] for j in range(blocks)], axis=1)


def half_kernel(core, held, weight, pairs, ahead, mine, sems):
    chips = held.shape[0]
    blocks = weight.shape[1] // HEAD
    rows = pairs.shape[0]
    loads = [pltpu.make_async_copy(weight.at[2 * x + core[0]], mine.at[x], sems.at[x]) for x in range(chips)]
    more = [
        pltpu.make_async_copy(weight.at[2 * x + 1 - core[0]], ahead.at[x], sems.at[chips + x])
        for x in range(chips)
    ]
    for load in loads + more:
        load.start()
    total = jnp.zeros(pairs.shape, jnp.float32)
    for x in range(chips):
        loads[x].wait()
        total = total + exact(gathered(held, x, rows, blocks), mine[x])
    pairs[...] = total
    for load in more:
        load.wait()


def finish_kernel(reqs, scale, mine, other, pairs, weight, queries, old, table, out_attn, out_kv):
    rows = queries.shape[0]
    chips = mine.shape[0]
    blocks = weight.shape[1] // HEAD
    squares = jnp.zeros((EXTRA, HEAD), jnp.float32)
    for held in (mine, other):
        for x in range(chips):
            squares = squares + held[x, rows * blocks : rows * blocks + EXTRA, :].astype(jnp.float32)
    squares = jnp.sum(squares, axis=0, keepdims=True)
    squares = jnp.sum(jnp.where(diagonal(rows), squares, 0.0), axis=-1, keepdims=True)
    inverse = lax.rsqrt(squares / D + EPSILON)
    pairs = pairs[...]
    for x in range(chips):
        pairs = pairs + exact(gathered(other, x, rows, blocks), weight[x])
    pairs = pairs * inverse
    keys = pairs[:, :HEAD]
    turned = pltpu.roll(keys, HEAD // 2, 1)
    new_keys = (keys * table[0] + turned * table[1]).astype(jnp.bfloat16)
    new_values = pairs[:, HEAD:].astype(jnp.bfloat16)
    padding = jnp.zeros((HEAD - rows, HEAD), jnp.bfloat16)
    wide_keys = jnp.concatenate([new_keys, padding], axis=0)
    wide_values = jnp.concatenate([new_values, padding], axis=0)
    by, of = iota((rows, HEAD), 0), iota((rows, HEAD), 1)
    seen = (by % reqs == of % reqs) & (of // reqs <= by // reqs)
    live = table[2]
    groups = old.shape[0]
    asked = jnp.concatenate([queries[:, g * HEAD : (g + 1) * HEAD] for g in range(groups)], axis=0)
    scores = contract_last(asked, wide_keys)
    fresh, kept = [], []
    for g in range(groups):
        score = jnp.where(seen, scores[g * rows : (g + 1) * rows] * scale, -1e30)
        old_top = old[g, :, HEAD : 2 * HEAD]
        top = jnp.maximum(old_top, jnp.max(score, axis=-1, keepdims=True))
        shrink = jnp.exp(old_top - top)
        grown = jnp.exp(score - top)
        total = shrink * old[g, :, 2 * HEAD :] + jnp.sum(grown, axis=-1, keepdims=True)
        part = 1.0 / total
        fresh.append((grown * part).astype(jnp.bfloat16))
        kept.append(old[g, :, 0:HEAD] * (shrink * part))
    added = exact(jnp.concatenate(fresh, axis=0), wide_values)
    for g in range(groups):
        mixed = kept[g] + added[g * rows : (g + 1) * rows]
        out_attn[:, g * HEAD : (g + 1) * HEAD] = (mixed * live).astype(jnp.bfloat16)
    to, fro = iota((2 * rows, 2 * rows), 0), iota((2 * rows, 2 * rows), 1)
    weave = as_bf16(fro == (to // 2) + rows * (to % 2))
    stacked = jnp.concatenate([new_keys, new_values], axis=0)
    out_kv[...] = exact(weave, stacked).astype(jnp.bfloat16)


def far(x):
    return pltpu.with_memory_space_constraint(x, pltpu.HBM)


def near(x):
    return pltpu.with_memory_space_constraint(x, pltpu.VMEM)


def small(mebibytes):
    return pltpu.CompilerParams(vmem_limit_bytes=mebibytes << 20)


def spread(x, axis, groups=None):
    return lax.all_to_all(x, axis, 0, 0, axis_index_groups=groups)


def local(hidden, norm_gain, w_kv, queries, cache_kv, exits, lengths):
    num_steps, _, local_reqs, width = hidden.shape
    rows = num_steps * local_reqs
    slots = num_steps * EXIT_CAP
    sections = lax.axis_size("section")
    section_index = lax.axis_index("section")
    parts = lax.axis_size("tp")
    chips = parts // 2
    core = lax.axis_index("tp") % 2
    kv_local = w_kv.shape[-1]
    groups = queries.shape[-1] // kv_local
    scale = HEAD ** (-0.5)

    own = hidden.reshape(rows, width)
    flat_exits = exits.reshape(rows)
    section_scalar = section_index.reshape(1)
    outgoing = pl.pallas_call(
        leaving_kernel,
        out_shape=pltpu.HBM((sections, slots, width), jnp.bfloat16),
        in_specs=[SMEM, HBM, HBM],
        out_specs=HBM,
        scratch_shapes=[
            pltpu.VMEM(exits.shape, jnp.int32),
            pltpu.VMEM(own.shape, jnp.bfloat16),
            pltpu.VMEM((slots, width), jnp.bfloat16),
            pltpu.SemaphoreType.DMA((sections + 2,)),
        ],
        compiler_params=small(4),
        name="leaving",
    )(section_scalar, far(exits), far(own))
    arrived = spread(outgoing, "section").reshape(sections * slots, width)

    take, kept = pl.pallas_call(
        choose_kernel,
        out_shape=(
            pltpu.VMEM((rows, sections * slots), jnp.bfloat16),
            pltpu.VMEM((rows, width), jnp.bfloat16),
        ),
        in_specs=[SMEM, VMEM, VMEM],
        out_specs=(VMEM, VMEM),
        compiler_params=small(4),
        name="choose",
    )(section_scalar, exits, own)
    step_of = jnp.arange(num_steps, dtype=jnp.int32)[:, None]
    positions = (lengths[None, :] + step_of).reshape(rows)
    exponent = jnp.arange(HEAD // 2, dtype=jnp.float32) * (2.0 / HEAD)
    angles = positions.astype(jnp.float32)[:, None] * ROPE_BASE ** (-exponent)
    cosine, sine = jnp.cos(angles), jnp.sin(angles)
    live = (section_index < flat_exits).astype(jnp.float32)
    table = jnp.stack(
        [
            jnp.concatenate([cosine, cosine], axis=-1),
            jnp.concatenate([-sine, sine], axis=-1),
            jnp.broadcast_to(live[:, None], (rows, HEAD)),
        ]
    )
    by_request = queries.reshape(num_steps, local_reqs, groups, HEAD).transpose(1, 0, 2, 3)
    weight = pl.pallas_call(
        split_kernel,
        grid=(chips,),
        out_shape=pltpu.HBM((parts, width, 2 * HEAD), jnp.bfloat16),
        in_specs=[pl.BlockSpec((4 * width, HEAD), lambda i: (i, 0))],
        out_specs=pl.BlockSpec((2, width, 2 * HEAD), lambda i: (i, 0, 0)),
        scratch_shapes=[pltpu.VMEM((4 * width, HEAD), jnp.float32)],
        compiler_params=small(16),
        name="split",
    )(far(w_kv.reshape(2 * D, HEAD)))
    old = pl.pallas_call(
        lambda *refs: past_kernel(scale, *refs),
        out_shape=pltpu.VMEM((groups, rows, 3 * HEAD), jnp.float32),
        in_specs=[SMEM, VMEM, VMEM],
        out_specs=VMEM,
        compiler_params=small(8),
        name="past",
    )(lengths, near(by_request.reshape(rows * groups, HEAD)), near(cache_kv[0]))

    weight, old, table, take, kept, arrived = lax.optimization_barrier(
        (weight, old, table, take, kept, arrived)
    )
    sent = pl.pallas_call(
        place_kernel,
        out_shape=pltpu.VMEM((chips, rows * (width // HEAD) + EXTRA, HEAD), jnp.bfloat16),
        in_specs=[VMEM] * 4,
        out_specs=VMEM,
        compiler_params=small(4),
        name="place",
    )(near(take), near(kept), near(arrived), near(norm_gain))
    same_core = [[2 * x + c for x in range(chips)] for c in range(2)]
    mine = spread(sent, "tp", same_core)
    other = lax.ppermute(mine, "tp", [(i, i ^ 1) for i in range(parts)])

    pairs, ahead = pl.pallas_call(
        half_kernel,
        out_shape=(
            pltpu.VMEM((rows, 2 * HEAD), jnp.float32),
            pltpu.VMEM((chips, width, 2 * HEAD), jnp.bfloat16),
        ),
        in_specs=[SMEM, VMEM, HBM],
        out_specs=(VMEM, VMEM),
        scratch_shapes=[
            pltpu.VMEM((chips, width, 2 * HEAD), jnp.bfloat16),
            pltpu.SemaphoreType.DMA((parts,)),
        ],
        compiler_params=small(16),
        name="half",
    )(core.reshape(1), near(mine), far(weight))
    attended, fresh = pl.pallas_call(
        lambda *refs: finish_kernel(local_reqs, scale, *refs),
        out_shape=(
            jax.ShapeDtypeStruct((rows, groups * HEAD), jnp.bfloat16),
            jax.ShapeDtypeStruct((2 * rows, HEAD), jnp.bfloat16),
        ),
        in_specs=[VMEM] * 7,
        out_specs=(VMEM, VMEM),
        compiler_params=small(16),
        name="finish",
    )(
        near(mine),
        near(other),
        near(pairs),
        near(ahead),
        near(queries.reshape(rows, groups * HEAD)),
        near(old),
        near(table),
    )
    return (
        attended.reshape(num_steps, 1, local_reqs, groups * HEAD),
        fresh.reshape(num_steps, 1, local_reqs, 2, kv_local),
    )


def solution(mesh):
    placed = (
        P(None, "section", "req", "tp"),
        P("section", "tp"),
        P("section", None, None, "tp"),
        P(None, "section", "req", "tp"),
        P("section", "req", None, None, "tp"),
        P(None, "req"),
        P("req"),
    )
    return jax.shard_map(
        local,
        mesh=mesh,
        in_specs=placed,
        out_specs=(P(None, "section", "req", "tp"), P(None, "section", "req", None, "tp")),
        check_vma=False,
    )
```

```python
import jax
import jax.numpy as jnp
from jax import lax
from jax.experimental import pallas as pl
from jax.experimental.pallas import tpu as pltpu
from jax.sharding import PartitionSpec as P

D = 8192
HEAD = 128
EXIT_CAP = 2
EXTRA = 8
TURN = 8
CHIP_ORDER = (0,1,2,3)


EPSILON = 1e-05
ROPE_BASE = 500000.0
VMEM = pl.BlockSpec(memory_space=pltpu.VMEM)
SMEM = pl.BlockSpec(memory_space=pltpu.SMEM)
HBM = pl.BlockSpec(memory_space=pltpu.HBM)


def iota(shape, axis):
    return lax.broadcasted_iota(jnp.int32, shape, axis)


def contract_last(a, b):
    return lax.dot_general(a, b, (((1,), (1,)), ((), ())), preferred_element_type=jnp.float32)


def as_bf16(mask):
    return mask.astype(jnp.float32).astype(jnp.bfloat16)


def exact(a, b):
    return jnp.dot(a, b, preferred_element_type=jnp.float32)


def ranks(same):
    reqs = same.shape[1]
    before = iota((reqs, reqs), 0) < iota((reqs, reqs), 1)
    return exact(as_bf16(same), as_bf16(before))


def leaving_kernel(section, exits_far, own_far, out, exits, own, chosen, sems):
    steps, reqs = exits.shape
    rows = own.shape[0]
    copies = out.shape[0]
    load_exits = pltpu.make_async_copy(exits_far, exits, sems.at[copies])
    load_own = pltpu.make_async_copy(own_far, own, sems.at[copies + 1])
    load_exits.start()
    load_own.start()
    load_exits.wait()
    here = exits[...] == section[0]
    rank = ranks(here)
    picks = [here & (rank == k) for k in range(EXIT_CAP)]
    picks = jnp.concatenate([pick.astype(jnp.float32) for pick in picks], axis=0)
    widen = as_bf16(iota((reqs, rows), 0) == iota((reqs, rows), 1) % reqs)
    wide = exact(picks.astype(jnp.bfloat16), widen)
    slots = EXIT_CAP * steps
    match = iota((slots, rows), 0) % steps == iota((slots, rows), 1) // reqs
    wide = jnp.where(match, wide, 0.0).astype(jnp.bfloat16)
    load_own.wait()
    chosen[...] = exact(wide, own[...]).astype(jnp.bfloat16)
    stores = [pltpu.make_async_copy(chosen, out.at[k], sems.at[k]) for k in range(copies)]
    for store in stores:
        store.start()
    for store in stores:
        store.wait()


def choose_kernel(section, exits, own, take, kept):
    steps, reqs = exits.shape
    rows, reach = take.shape
    slots = EXIT_CAP * steps
    layer = exits[...]
    rank = jnp.zeros((steps, reqs), jnp.float32)
    for e in range(reach // slots):
        same = layer == e
        rank = jnp.where(same, ranks(same), rank)
    gone = layer < section[0]
    count = reach // slots
    slot = ((layer + count - TURN) % count) * slots + rank.astype(jnp.int32) * steps + iota((steps, reqs), 0)
    slot = jnp.where(gone, slot, -1).astype(jnp.float32)
    spread_steps = as_bf16(iota((rows, steps), 0) // reqs == iota((rows, steps), 1))
    column = exact(spread_steps, slot.astype(jnp.bfloat16))
    own_lane = iota((rows, reqs), 0) % reqs == iota((rows, reqs), 1)
    column = jnp.sum(jnp.where(own_lane, column, 0.0), axis=-1, keepdims=True)
    take[...] = as_bf16(column.astype(jnp.int32) == iota((rows, reach), 1))
    kept[...] = jnp.where(column >= 0.0, 0.0, own[...].astype(jnp.float32)).astype(jnp.bfloat16)


def split_kernel(weight, out, wide):
    rows = weight.shape[0] // 2
    wide[...] = weight[...].astype(jnp.float32)
    for k in range(2):
        half = wide[pl.ds(k, rows, stride=2), :].astype(jnp.bfloat16)
        for p in range(out.shape[0]):
            part = half[p * out.shape[1] : (p + 1) * out.shape[1]]
            out[p, :, HEAD * k : HEAD * (k + 1)] = part


def past_kernel(scale, lengths, queries, cache, out):
    reqs = cache.shape[0]
    per = queries.shape[0] // reqs
    groups = out.shape[0]
    for r in range(reqs):
        scores = contract_last(queries[r * per : (r + 1) * per, :], cache[r, 0]) * scale
        scores = jnp.where(iota(scores.shape, 1) < lengths[r], scores, -1e30)
        top = jnp.max(scores, axis=-1, keepdims=True)
        grown = jnp.exp(scores - top)
        total = jnp.sum(grown, axis=-1, keepdims=True)
        high = grown.astype(jnp.bfloat16)
        low = (grown - high.astype(jnp.float32)).astype(jnp.bfloat16)
        mixed = exact(high, cache[r, 1]) + exact(low, cache[r, 1])
        top = jnp.broadcast_to(top, (per, HEAD))
        total = jnp.broadcast_to(total, (per, HEAD))
        for t in range(per // groups):
            row = slice(t * reqs + r, t * reqs + r + 1)
            for g in range(groups):
                at = slice(t * groups + g, t * groups + g + 1)
                out[g, row, 0:HEAD] = mixed[at]
                out[g, row, HEAD : 2 * HEAD] = top[at]
                out[g, row, 2 * HEAD : 3 * HEAD] = total[at]


def diagonal(rows):
    return iota((rows, HEAD), 0) == iota((rows, HEAD), 1)


def place_kernel(take, kept, arrived, gain, out):
    rows, width = kept.shape
    blocks = width // HEAD
    source = exact(take[...], arrived[...])
    source = (source + kept[...].astype(jnp.float32)).astype(jnp.bfloat16)
    values = source.astype(jnp.float32)
    squares = jnp.zeros((rows, HEAD), jnp.float32)
    for j in range(blocks):
        value = values[:, HEAD * j : HEAD * (j + 1)]
        squares = squares + value * value
    squares = jnp.sum(squares, axis=-1, keepdims=True)
    squares = jnp.sum(jnp.where(diagonal(rows), squares, 0.0), axis=0, keepdims=True)
    high = squares.astype(jnp.bfloat16).astype(jnp.float32)
    middle = (squares - high).astype(jnp.bfloat16).astype(jnp.float32)
    low = squares - high - middle
    at = iota((EXTRA, HEAD), 0)
    sums = jnp.zeros((EXTRA, HEAD), jnp.float32)
    for k, piece in enumerate((high, middle, low)):
        sums = jnp.where(at == k, piece, sums)
    scaled = (values * gain[...].astype(jnp.float32)).astype(jnp.bfloat16)
    extra = sums.astype(jnp.bfloat16)
    for k in range(out.shape[0]):
        for j in range(blocks):
            out[k, rows * j : rows * (j + 1), :] = scaled[:, HEAD * j : HEAD * (j + 1)]
        out[k, rows * blocks : rows * blocks + EXTRA, :] = extra


def gathered(held, x, rows, blocks):
    return jnp.concatenate([held[x, rows * j : rows * (j + 1), :] for j in range(blocks)], axis=1)


def half_kernel(core, held, weight, pairs, ahead, mine, sems):
    chips = held.shape[0]
    blocks = weight.shape[1] // HEAD
    rows = pairs.shape[0]
    loads = [
        pltpu.make_async_copy(weight.at[2 * CHIP_ORDER[x] + core[0]], mine.at[x], sems.at[x])
        for x in range(chips)
    ]
    more = [
        pltpu.make_async_copy(weight.at[2 * CHIP_ORDER[x] + 1 - core[0]], ahead.at[x], sems.at[chips + x])
        for x in range(chips)
    ]
    for load in loads + more:
        load.start()
    total = jnp.zeros(pairs.shape, jnp.float32)
    for x in range(chips):
        loads[x].wait()
        total = total + exact(gathered(held, x, rows, blocks), mine[x])
    pairs[...] = total
    for load in more:
        load.wait()


def finish_kernel(reqs, scale, mine, other, pairs, weight, queries, old, table, out_attn, out_kv):
    rows = queries.shape[0]
    chips = mine.shape[0]
    blocks = weight.shape[1] // HEAD
    squares = jnp.zeros((EXTRA, HEAD), jnp.float32)
    for held in (mine, other):
        for x in range(chips):
            squares = squares + held[x, rows * blocks : rows * blocks + EXTRA, :].astype(jnp.float32)
    squares = jnp.sum(squares, axis=0, keepdims=True)
    squares = jnp.sum(jnp.where(diagonal(rows), squares, 0.0), axis=-1, keepdims=True)
    inverse = lax.rsqrt(squares / D + EPSILON)
    pairs = pairs[...]
    for x in range(chips):
        pairs = pairs + exact(gathered(other, x, rows, blocks), weight[x])
    pairs = pairs * inverse
    keys = pairs[:, :HEAD]
    turned = pltpu.roll(keys, HEAD // 2, 1)
    new_keys = (keys * table[0] + turned * table[1]).astype(jnp.bfloat16)
    new_values = pairs[:, HEAD:].astype(jnp.bfloat16)
    padding = jnp.zeros((HEAD - rows, HEAD), jnp.bfloat16)
    wide_keys = jnp.concatenate([new_keys, padding], axis=0)
    wide_values = jnp.concatenate([new_values, padding], axis=0)
    by, of = iota((rows, HEAD), 0), iota((rows, HEAD), 1)
    seen = (by % reqs == of % reqs) & (of // reqs <= by // reqs)
    live = table[2]
    groups = old.shape[0]
    asked = jnp.concatenate([queries[:, g * HEAD : (g + 1) * HEAD] for g in range(groups)], axis=0)
    scores = contract_last(asked, wide_keys)
    fresh, kept = [], []
    for g in range(groups):
        score = jnp.where(seen, scores[g * rows : (g + 1) * rows] * scale, -1e30)
        old_top = old[g, :, HEAD : 2 * HEAD]
        top = jnp.maximum(old_top, jnp.max(score, axis=-1, keepdims=True))
        shrink = jnp.exp(old_top - top)
        grown = jnp.exp(score - top)
        total = shrink * old[g, :, 2 * HEAD :] + jnp.sum(grown, axis=-1, keepdims=True)
        part = 1.0 / total
        fresh.append((grown * part).astype(jnp.bfloat16))
        kept.append(old[g, :, 0:HEAD] * (shrink * part))
    added = exact(jnp.concatenate(fresh, axis=0), wide_values)
    for g in range(groups):
        mixed = kept[g] + added[g * rows : (g + 1) * rows]
        out_attn[:, g * HEAD : (g + 1) * HEAD] = (mixed * live).astype(jnp.bfloat16)
    to, fro = iota((2 * rows, 2 * rows), 0), iota((2 * rows, 2 * rows), 1)
    weave = as_bf16(fro == (to // 2) + rows * (to % 2))
    stacked = jnp.concatenate([new_keys, new_values], axis=0)
    out_kv[...] = exact(weave, stacked).astype(jnp.bfloat16)


def far(x):
    return pltpu.with_memory_space_constraint(x, pltpu.HBM)


def near(x):
    return pltpu.with_memory_space_constraint(x, pltpu.VMEM)


def small(mebibytes):
    return pltpu.CompilerParams(vmem_limit_bytes=mebibytes << 20)


def spread(x, axis, groups=None):
    return lax.all_to_all(x, axis, 0, 0, axis_index_groups=groups)


def local(hidden, norm_gain, w_kv, queries, cache_kv, exits, lengths):
    num_steps, _, local_reqs, width = hidden.shape
    rows = num_steps * local_reqs
    slots = num_steps * EXIT_CAP
    sections = lax.axis_size("section")
    section_index = lax.axis_index("section")
    parts = lax.axis_size("tp")
    chips = parts // 2
    core = lax.axis_index("tp") % 2
    kv_local = w_kv.shape[-1]
    groups = queries.shape[-1] // kv_local
    scale = HEAD ** (-0.5)

    own = hidden.reshape(rows, width)
    flat_exits = exits.reshape(rows)
    section_scalar = section_index.reshape(1)
    outgoing = pl.pallas_call(
        leaving_kernel,
        out_shape=pltpu.HBM((sections, slots, width), jnp.bfloat16),
        in_specs=[SMEM, HBM, HBM],
        out_specs=HBM,
        scratch_shapes=[
            pltpu.VMEM(exits.shape, jnp.int32),
            pltpu.VMEM(own.shape, jnp.bfloat16),
            pltpu.VMEM((slots, width), jnp.bfloat16),
            pltpu.SemaphoreType.DMA((sections + 2,)),
        ],
        compiler_params=small(4),
        name="leaving",
    )(section_scalar, far(exits), far(own))
    ring = [[(k + TURN) % sections for k in range(sections)]]
    arrived = spread(outgoing, "section", ring).reshape(sections * slots, width)

    take, kept = pl.pallas_call(
        choose_kernel,
        out_shape=(
            pltpu.VMEM((rows, sections * slots), jnp.bfloat16),
            pltpu.VMEM((rows, width), jnp.bfloat16),
        ),
        in_specs=[SMEM, VMEM, VMEM],
        out_specs=(VMEM, VMEM),
        compiler_params=small(4),
        name="choose",
    )(section_scalar, exits, own)
    step_of = jnp.arange(num_steps, dtype=jnp.int32)[:, None]
    positions = (lengths[None, :] + step_of).reshape(rows)
    exponent = jnp.arange(HEAD // 2, dtype=jnp.float32) * (2.0 / HEAD)
    angles = positions.astype(jnp.float32)[:, None] * ROPE_BASE ** (-exponent)
    cosine, sine = jnp.cos(angles), jnp.sin(angles)
    live = (section_index < flat_exits).astype(jnp.float32)
    table = jnp.stack(
        [
            jnp.concatenate([cosine, cosine], axis=-1),
            jnp.concatenate([-sine, sine], axis=-1),
            jnp.broadcast_to(live[:, None], (rows, HEAD)),
        ]
    )
    by_request = queries.reshape(num_steps, local_reqs, groups, HEAD).transpose(1, 0, 2, 3)
    weight = pl.pallas_call(
        split_kernel,
        grid=(chips,),
        out_shape=pltpu.HBM((parts, width, 2 * HEAD), jnp.bfloat16),
        in_specs=[pl.BlockSpec((4 * width, HEAD), lambda i: (i, 0))],
        out_specs=pl.BlockSpec((2, width, 2 * HEAD), lambda i: (i, 0, 0)),
        scratch_shapes=[pltpu.VMEM((4 * width, HEAD), jnp.float32)],
        compiler_params=small(16),
        name="split",
    )(far(w_kv.reshape(2 * D, HEAD)))
    old = pl.pallas_call(
        lambda *refs: past_kernel(scale, *refs),
        out_shape=pltpu.VMEM((groups, rows, 3 * HEAD), jnp.float32),
        in_specs=[SMEM, VMEM, VMEM],
        out_specs=VMEM,
        compiler_params=small(8),
        name="past",
    )(lengths, near(by_request.reshape(rows * groups, HEAD)), near(cache_kv[0]))

    weight, old, table, take, kept, arrived = lax.optimization_barrier(
        (weight, old, table, take, kept, arrived)
    )
    sent = pl.pallas_call(
        place_kernel,
        out_shape=pltpu.VMEM((chips, rows * (width // HEAD) + EXTRA, HEAD), jnp.bfloat16),
        in_specs=[VMEM] * 4,
        out_specs=VMEM,
        compiler_params=small(4),
        name="place",
    )(near(take), near(kept), near(arrived), near(norm_gain))
    same_core = [[2 * x + c for x in CHIP_ORDER] for c in range(2)]
    mine = spread(sent, "tp", same_core)
    other = lax.ppermute(mine, "tp", [(i, i ^ 1) for i in range(parts)])

    pairs, ahead = pl.pallas_call(
        half_kernel,
        out_shape=(
            pltpu.VMEM((rows, 2 * HEAD), jnp.float32),
            pltpu.VMEM((chips, width, 2 * HEAD), jnp.bfloat16),
        ),
        in_specs=[SMEM, VMEM, HBM],
        out_specs=(VMEM, VMEM),
        scratch_shapes=[
            pltpu.VMEM((chips, width, 2 * HEAD), jnp.bfloat16),
            pltpu.SemaphoreType.DMA((parts,)),
        ],
        compiler_params=small(16),
        name="half",
    )(core.reshape(1), near(mine), far(weight))
    attended, fresh = pl.pallas_call(
        lambda *refs: finish_kernel(local_reqs, scale, *refs),
        out_shape=(
            jax.ShapeDtypeStruct((rows, groups * HEAD), jnp.bfloat16),
            jax.ShapeDtypeStruct((2 * rows, HEAD), jnp.bfloat16),
        ),
        in_specs=[VMEM] * 7,
        out_specs=(VMEM, VMEM),
        compiler_params=small(16),
        name="finish",
    )(
        near(mine),
        near(other),
        near(pairs),
        near(ahead),
        near(queries.reshape(rows, groups * HEAD)),
        near(old),
        near(table),
    )
    return (
        attended.reshape(num_steps, 1, local_reqs, groups * HEAD),
        fresh.reshape(num_steps, 1, local_reqs, 2, kv_local),
    )


def solution(mesh):
    placed = (
        P(None, "section", "req", "tp"),
        P("section", "tp"),
        P("section", None, None, "tp"),
        P(None, "section", "req", "tp"),
        P("section", "req", None, None, "tp"),
        P(None, "req"),
        P("req"),
    )
    return jax.shard_map(
        local,
        mesh=mesh,
        in_specs=placed,
        out_specs=(P(None, "section", "req", "tp"), P(None, "section", "req", None, "tp")),
        check_vma=False,
    )
```
